32 devices in a mesh: dp: 8 (over z, x), tensor: 4 (over y, core).
Axes of the slice: x: 2, y: 2, z: 4, core: 2. Of those that a mesh axis runs over, the one named last changes fastest.
Arguments:
- tokens: bfloat16 [8192, 640], P('dp'), may hold values from -6 to 6
- segment_ids: int32 [8, 1024], P('dp'), may hold values from 0 to 3, never falling along the last dimension, each value on 1 to 768 neighbouring positions
- input_gain: float32 [640], replicated, may hold values from -0.5 to 0.5
- q_weight: bfloat16 [640, 1024], P(None, 'tensor'), as said below
- k_weight: bfloat16 [640, 256], replicated, as said below
- v_weight: bfloat16 [640, 256], replicated, may hold values from -0.25 to 0.25
- query_gain: float32 [256], replicated, as said below
- key_gain: float32 [256], replicated, as said below
- o_weight: bfloat16 [640, 1024], P(None, 'tensor'), may hold values from -0.1875 to 0.1875
- post_attn_gain: float32 [640], replicated, may hold values from -0.5 to 0.5
- pre_ffn_gain: float32 [640], replicated, may hold values from -0.5 to 0.5
- gate_weight: bfloat16 [640, 2048], P(None, 'tensor'), may hold values from -0.25 to 0.25
- up_weight: bfloat16 [640, 2048], P(None, 'tensor'), may hold values from -0.25 to 0.25
- down_weight: bfloat16 [640, 2048], P(None, 'tensor'), may hold values from -0.125 to 0.125
- post_ffn_gain: float32 [640], replicated, may hold values from -0.5 to 0.5
- out_grad: bfloat16 [8192, 640], P('dp'), may hold values from -6 to 6
Outputs:
- output: bfloat16 [8192, 640], P('dp')
- grad_tokens: float32 [8192, 640], P('dp')
- grad_input_gain: float32 [640], replicated
- grad_q_weight: float32 [640, 1024], P('dp', 'tensor')
- grad_k_weight: float32 [640, 256], P('dp')
- grad_v_weight: float32 [640, 256], P('dp')
- grad_query_gain: float32 [256], replicated
- grad_key_gain: float32 [256], replicated
- grad_o_weight: float32 [640, 1024], P('dp', 'tensor')
- grad_post_attn_gain: float32 [640], replicated
- grad_pre_ffn_gain: float32 [640], replicated
- grad_gate_weight: float32 [640, 2048], P('dp', 'tensor')
- grad_up_weight: float32 [640, 2048], P('dp', 'tensor')
- grad_down_weight: float32 [640, 2048], P('dp', 'tensor')
- grad_post_ffn_gain: float32 [640], replicated
The draws below stay inside these ranges and needn't reach their ends.
Inputs may be any that keep to these rules, and one draw needn't show every extreme that they name: `segment_ids`: along each row numbers never fall; a run of equal numbers is one document. `q_weight`: entries lie within -0.25 to 0.25. `k_weight`: entries lie within -0.25 to 0.25. `query_gain`: entries lie within -0.5 to 2.5. `key_gain`: entries lie within -0.5 to 2.5.
All inputs are finite; a program needn't handle non-finite values.
Results may differ from the reference program's by a relative error of at most 0.034.
The reference program's roundings to bfloat16 on the way count: a program that leaves them out, or rounds other values in their place, can miss the bound.
Values may be sent and summed in bfloat16 or wider, within the bound.
A program may use at most 128 MiB of HBM per device.

```python
import math
import jax
import jax.numpy as jnp
import numpy as np
from jax import lax

D = 640
NH = 4
HD = 256
FF = 2048
WIN = 512
SEGS = 4
TOK_DEV = 1024
QW = 1024
TOKENS = 8192
N_DP = 8
N_TENSOR = 4


def shared_projections(key):
    query_base = jax.random.normal(jax.random.fold_in(key, 101), (D, NH * HD), jnp.float32)
    key_noise = jax.random.normal(jax.random.fold_in(key, 102), (D, HD), jnp.float32)
    return (query_base, key_noise)


def draw_q_weight(key, part):
    query_base, key_noise = shared_projections(key)
    return jnp.clip(query_base * D ** (-0.5), -0.25, 0.25).astype(jnp.bfloat16)


def draw_k_weight(key, part):
    query_base, key_noise = shared_projections(key)
    combined = key_noise
    return jnp.clip(combined * D ** (-0.5), -0.25, 0.25).astype(jnp.bfloat16)


def draw_query_gain(key, part):
    local_key = jax.random.fold_in(key, 201)
    return jax.random.uniform(local_key, (HD,), jnp.float32, -0.5, 0.5)


def draw_key_gain(key, part):
    local_key = jax.random.fold_in(key, 202)
    return jax.random.uniform(local_key, (HD,), jnp.float32, -0.5, 0.5)


def raised(values, stream_key, source, target, blocks, factor):
    owner, partner = [(jnp.arange(values.shape[dim]) // (values.shape[dim] // blocks)).reshape([-1 if axis == dim else 1 for axis in range(values.ndim)]) for dim in (source, target)]
    chosen = jax.random.permutation(stream_key, blocks)[partner]
    strong = (owner == chosen) | (owner == (partner + blocks // 2) % blocks)
    return jnp.where(strong, factor * values, values)


def block_levels(rng, dims, shards, least, high):
    factor_of, own = 1.0, jax.random.fold_in(rng, 6)
    for axis_at, parts in shards:
        heights = jnp.exp(jax.random.uniform(jax.random.fold_in(own, axis_at), (parts,), jnp.float32, least / len(shards), high / len(shards)))
        factor_of = factor_of * jnp.repeat(heights, dims[axis_at] // parts).reshape([-1 if axis == axis_at else 1 for axis in range(len(dims))])
    return factor_of


def length_profile(amount, total, bound, skew):
    portions = [(1 << 20) // math.isqrt(standing ** skew) + 1 for standing in range(2, amount + 1)]
    rest, given = total - bound - (amount - 1), [1] * (amount - 1)
    while rest > 0:
        movable = [i for i in range(amount - 1) if given[i] < bound]
        whole, budget = sum([portions[i] for i in movable]), rest
        for i in movable:
            addition = min(bound - given[i], max(1, budget * portions[i] // whole), rest)
            given[i] = given[i] + addition
            rest = rest - addition
    return np.array([bound] + given)


def uneven_parts(key, amount, total, limit, slope):
    if amount == 2:
        one = jax.random.randint(key, (), max(1, total - limit), min(limit, total - 1) + 1)
        return jnp.stack([one, total - one])
    tallies = jnp.asarray(length_profile(amount, total, limit, slope), jnp.int32)
    couples = (amount - 1) // 2
    giver, receiver = tallies[1:1 + 2 * couples:2], tallies[2:2 + 2 * couples:2]
    margin = jnp.minimum(giver - 1, limit - receiver)
    shifted = jax.random.randint(jax.random.fold_in(key, 1), (couples,), 0, 1 << 20) % (margin + 1)
    tallies = tallies.at[1:1 + 2 * couples:2].set(giver - shifted).at[2:2 + 2 * couples:2].set(receiver + shifted)
    return tallies[jax.random.permutation(jax.random.fold_in(key, 2), amount)]


def bell_draw(own_key, extent, deviation, bound, cuts=(), held_as=jnp.bfloat16):
    values = jax.random.normal(own_key, extent, jnp.float32) * deviation
    if len(cuts) > 0:
        values = block_levels(own_key, extent, cuts, -0.22, 0.18) * values
    return jnp.clip(values, min=-bound, max=bound).astype(held_as)


def bell_draw_with(key, dims, spread, limit, shards, heavy, kind=jnp.bfloat16):
    drawn = spread * jax.random.normal(key, dims, jnp.float32)
    if shards:
        drawn = drawn * block_levels(key, dims, shards, -0.22, 0.18)
    return jnp.clip(raised(drawn, jax.random.fold_in(key, 3), *heavy), -limit, limit).astype(kind)


def setup_inputs(seed: int = 0) -> dict:
    seeds = jax.random.split(jax.random.key(seed), 17)
    tokens = bell_draw_with(seeds[0], (TOKENS, D), 1.0, 6.0, ((0, 8),), (0, 1, 8, 2.0))
    segment_ids = jax.vmap(lambda own: jnp.searchsorted(jnp.cumsum(uneven_parts(own, SEGS, TOK_DEV, 3 * TOK_DEV // 4, 1)), jnp.arange(TOK_DEV), side="right"))(jax.random.split(seeds[1], N_DP)).reshape((N_DP, TOK_DEV)).astype(jnp.int32)
    input_gain = jnp.clip(jax.random.uniform(seeds[2], (D,), jnp.float32, -0.5, 0.5), -0.5, 0.5)
    q_weight = draw_q_weight(jax.random.fold_in(seeds[16], 71), 0)
    k_weight = draw_k_weight(jax.random.fold_in(seeds[16], 71), 0)
    v_weight = bell_draw(seeds[5], (D, HD), D ** -0.5, 0.25)
    query_gain = draw_query_gain(jax.random.fold_in(seeds[16], 71), 0)
    key_gain = draw_key_gain(jax.random.fold_in(seeds[16], 71), 0)
    o_weight = bell_draw(seeds[8], (D, QW), QW ** -0.5, 0.1875, ((1, 4),))
    post_attn_gain = jnp.clip(jax.random.uniform(seeds[9], (D,), jnp.float32, -0.5, 0.5), -0.5, 0.5)
    pre_ffn_gain = jnp.clip(jax.random.uniform(seeds[10], (D,), jnp.float32, -0.5, 0.5), -0.5, 0.5)
    gate_weight = bell_draw(seeds[11], (D, FF), D ** -0.5, 0.25, ((1, 4),))
    up_weight = bell_draw(seeds[12], (D, FF), D ** -0.5, 0.25, ((1, 4),))
    down_weight = bell_draw(seeds[13], (D, FF), FF ** -0.5, 0.125, ((1, 4),))
    post_ffn_gain = jnp.clip(jax.random.uniform(seeds[14], (D,), jnp.float32, -0.5, 0.5), -0.5, 0.5)
    out_grad = bell_draw_with(seeds[15], (TOKENS, D), 1.0, 6.0, ((0, 8),), (0, 1, 8, 2.0))
    return {"tokens": tokens, "segment_ids": segment_ids, "input_gain": input_gain, "q_weight": q_weight, "k_weight": k_weight, "v_weight": v_weight, "query_gain": query_gain, "key_gain": key_gain, "o_weight": o_weight, "post_attn_gain": post_attn_gain, "pre_ffn_gain": pre_ffn_gain, "gate_weight": gate_weight, "up_weight": up_weight, "down_weight": down_weight, "post_ffn_gain": post_ffn_gain, "out_grad": out_grad}


norm_eps = 1e-06
rope_base = 10000.0
gelu_coef = 0.7978845608028654
cube_coef = 0.044715
masked_value = -1e+30

def widen(values):
    return lax.optimization_barrier(values).astype(jnp.float32)

def round_trip(values):
    return lax.optimization_barrier(values.astype(jnp.bfloat16)).astype(jnp.float32)

def rms_forward(values, gain_vec):
    inverse = lax.rsqrt(lax.optimization_barrier(jnp.mean(values * values, axis=-1, keepdims=True)) + norm_eps)
    unit_vals = values * inverse
    return (unit_vals * (1.0 + gain_vec), unit_vals, inverse)

def rms_backward(grad_vals, unit_vals, inverse, gain_vec):
    scaled = grad_vals * (1.0 + gain_vec)
    return inverse * (scaled - unit_vals * lax.optimization_barrier(jnp.mean(scaled * unit_vals, axis=-1, keepdims=True)))

def doc_positions(segment_row):
    row_count = segment_row.shape[0]
    row_index = jnp.arange(row_count, dtype=jnp.int32)
    change = jnp.concatenate([jnp.ones((1,), dtype=jnp.bool_), segment_row[1:] != segment_row[:-1]])
    starts = lax.cummax(jnp.where(change, row_index, 0).astype(jnp.int32), axis=0)
    return row_index - starts

def rope_tables(positions, head_dim):
    half_dim = head_dim // 2
    frequency = rope_base ** (-(jnp.arange(half_dim, dtype=jnp.float32) * 2.0 / head_dim))
    angles = positions.astype(jnp.float32)[:, None] * frequency[None, :]
    return (jnp.cos(angles), jnp.sin(angles))

def rotate(values, cosine, sine_tab):
    half_dim = values.shape[-1] // 2
    first_half = values[..., :half_dim]
    second_half = values[..., half_dim:]
    cos_b = cosine[:, None, :]
    sin_b = sine_tab[:, None, :]
    return jnp.concatenate([first_half * cos_b - second_half * sin_b, second_half * cos_b + first_half * sin_b], axis=-1)

def unrotate(values, cosine, sine_tab):
    half_dim = values.shape[-1] // 2
    first_half = values[..., :half_dim]
    second_half = values[..., half_dim:]
    cos_b = cosine[:, None, :]
    sin_b = sine_tab[:, None, :]
    return jnp.concatenate([first_half * cos_b + second_half * sin_b, second_half * cos_b - first_half * sin_b], axis=-1)

def gelu_parts(gate_pre):
    inner_arg = gelu_coef * (gate_pre + cube_coef * gate_pre * gate_pre * gate_pre)
    tanh_val = jnp.tanh(inner_arg)
    gelu_value = 0.5 * gate_pre * (1.0 + tanh_val)
    gelu_slope = 0.5 * (1.0 + tanh_val) + 0.5 * gate_pre * (1.0 - tanh_val * tanh_val) * gelu_coef * (1.0 + 3.0 * cube_coef * gate_pre * gate_pre)
    return (gelu_value, gelu_slope)

def window_mask(query_seg, key_seg, block_rows, window):
    row_ids = jnp.arange(block_rows, dtype=jnp.int32)[:, None]
    col_ids = jnp.arange(block_rows + window, dtype=jnp.int32)[None, :]
    inside = (col_ids > row_ids) & (col_ids <= row_ids + window)
    return inside & (query_seg[:, None] == key_seg[None, :])

def padded_inputs(key_rows, value_rows, segments, window):
    head_dim = key_rows.shape[-1]
    pad_keys = jnp.concatenate([jnp.zeros((window, head_dim), key_rows.dtype), key_rows], axis=0)
    pad_values = jnp.concatenate([jnp.zeros((window, head_dim), value_rows.dtype), value_rows], axis=0)
    pad_segments = jnp.concatenate([jnp.full((window,), -1, jnp.int32), segments.astype(jnp.int32)], axis=0)
    return (pad_keys, pad_values, pad_segments)

def attend_forward(query_rows, key_rows, value_rows, segments, window, block_rows):
    tok_count, head_count, head_dim = query_rows.shape
    score_scale = head_dim ** (-0.5)
    pad_keys, pad_values, pad_segments = padded_inputs(key_rows, value_rows, segments, window)
    key_span = block_rows + window

    def one_block(row_start):
        query_blk = lax.dynamic_slice_in_dim(query_rows, row_start, block_rows, 0)
        key_blk = lax.dynamic_slice_in_dim(pad_keys, row_start, key_span, 0)
        value_blk = lax.dynamic_slice_in_dim(pad_values, row_start, key_span, 0)
        allowed = window_mask(lax.dynamic_slice_in_dim(segments, row_start, block_rows, 0), lax.dynamic_slice_in_dim(pad_segments, row_start, key_span, 0), block_rows, window)
        scores = jnp.einsum('bhd,kd->hbk', widen(query_blk), widen(key_blk)) * score_scale
        row_max = lax.optimization_barrier(jnp.max(jnp.where(allowed, scores, masked_value), axis=-1, keepdims=True))
        exp_vals = jnp.exp(jnp.where(allowed, scores - row_max, masked_value))
        row_total = lax.optimization_barrier(jnp.sum(exp_vals, axis=-1, keepdims=True))
        prob_bf = (exp_vals / row_total).astype(jnp.bfloat16)
        result = jnp.einsum('hbk,kd->bhd', widen(prob_bf), widen(value_blk)).astype(jnp.bfloat16)
        return (result, (row_max + jnp.log(row_total))[..., 0])
    starts = jnp.arange(tok_count // block_rows, dtype=jnp.int32) * block_rows
    results, lse_blocks = lax.map(one_block, starts)
    return (results.reshape(tok_count, head_count, head_dim), jnp.transpose(lse_blocks, (1, 0, 2)).reshape(head_count, tok_count))

def attend_backward(query_rows, key_rows, value_rows, attn_out, grad_attn, lse_rows, segments, window, block_rows):
    tok_count, head_count, head_dim = query_rows.shape
    score_scale = head_dim ** (-0.5)
    pad_keys, pad_values, pad_segments = padded_inputs(key_rows, value_rows, segments, window)
    key_span = block_rows + window
    delta_rows = jnp.transpose(lax.optimization_barrier(jnp.sum(widen(grad_attn) * widen(attn_out), axis=-1)))

    def one_block(carry, row_start):
        grad_keys, grad_values = carry
        query_blk = lax.dynamic_slice_in_dim(query_rows, row_start, block_rows, 0)
        key_blk = lax.dynamic_slice_in_dim(pad_keys, row_start, key_span, 0)
        value_blk = lax.dynamic_slice_in_dim(pad_values, row_start, key_span, 0)
        allowed = window_mask(lax.dynamic_slice_in_dim(segments, row_start, block_rows, 0), lax.dynamic_slice_in_dim(pad_segments, row_start, key_span, 0), block_rows, window)
        scores = jnp.einsum('bhd,kd->hbk', widen(query_blk), widen(key_blk)) * score_scale
        lse_blk = lax.dynamic_slice_in_dim(lse_rows, row_start, block_rows, 1)
        probs = jnp.exp(jnp.where(allowed, scores - lse_blk[..., None], masked_value))
        grad_blk = lax.dynamic_slice_in_dim(grad_attn, row_start, block_rows, 0)
        grad_probs = jnp.einsum('bhd,kd->hbk', widen(grad_blk), widen(value_blk))
        delta_blk = lax.dynamic_slice_in_dim(delta_rows, row_start, block_rows, 1)
        grad_scores = (probs * (grad_probs - delta_blk[..., None]) * score_scale).astype(jnp.bfloat16)
        grad_query = jnp.einsum('hbk,kd->bhd', widen(grad_scores), widen(key_blk))
        key_part = jnp.einsum('hbk,bhd->khd', widen(grad_scores), widen(query_blk))
        value_part = jnp.einsum('hbk,bhd->khd', widen(probs.astype(jnp.bfloat16)), widen(grad_blk))
        grad_keys = lax.dynamic_update_slice_in_dim(grad_keys, lax.dynamic_slice_in_dim(grad_keys, row_start, key_span, 0) + key_part, row_start, 0)
        grad_values = lax.dynamic_update_slice_in_dim(grad_values, lax.dynamic_slice_in_dim(grad_values, row_start, key_span, 0) + value_part, row_start, 0)
        return ((grad_keys, grad_values), grad_query)
    zeros_init = jnp.zeros((tok_count + window, head_count, head_dim), jnp.float32)
    starts = jnp.arange(tok_count // block_rows, dtype=jnp.int32) * block_rows
    (grad_keys, grad_values), grad_query = lax.scan(one_block, (zeros_init, zeros_init), starts)
    return (grad_query.reshape(tok_count, head_count, head_dim), grad_keys[window:], grad_values[window:])

def reference(tokens, segment_ids, input_gain, q_weight, k_weight, v_weight, query_gain, key_gain, o_weight, post_attn_gain, pre_ffn_gain, gate_weight, up_weight, down_weight, post_ffn_gain, out_grad):
    groups = N_TENSOR
    group_heads = NH // groups
    group_units = FF // groups
    block_rows = min(512, TOK_DEV)
    q_groups = q_weight.reshape(D, groups, group_heads * HD).astype(jnp.float32)
    o_groups = o_weight.reshape(D, groups, group_heads * HD).astype(jnp.float32)
    gate_groups = gate_weight.reshape(D, groups, group_units).astype(jnp.float32)
    up_groups = up_weight.reshape(D, groups, group_units).astype(jnp.float32)
    down_groups = down_weight.reshape(D, groups, group_units).astype(jnp.float32)
    k_wide = k_weight.astype(jnp.float32)
    v_wide = v_weight.astype(jnp.float32)
    contract_rows = (((0,), (0,)), ((), ()))

    def one_sequence(totals, inputs):
        tok_seq, seg_row, grad_seq = inputs
        positions = doc_positions(seg_row)
        cosine, sine_tab = rope_tables(positions, HD)
        tok_f32 = tok_seq.astype(jnp.float32)
        normed_in, unit_in, inv_in = rms_forward(tok_f32, input_gain)
        normed_in = normed_in.astype(jnp.bfloat16)
        query_raw = jnp.dot(normed_in, q_weight, preferred_element_type=jnp.float32).reshape(TOK_DEV, NH, HD)
        key_raw = jnp.dot(normed_in, k_weight, preferred_element_type=jnp.float32)
        value_bf = jnp.dot(normed_in, v_weight, preferred_element_type=jnp.float32).astype(jnp.bfloat16)
        query_normed, query_unit, query_inv = rms_forward(query_raw, query_gain)
        key_normed, key_unit, key_inv = rms_forward(key_raw, key_gain)
        query_rot = rotate(query_normed, cosine, sine_tab).astype(jnp.bfloat16)
        key_rot = rotate(key_normed[:, None, :], cosine, sine_tab)[:, 0, :].astype(jnp.bfloat16)
        attn_out, lse_rows = attend_forward(query_rot, key_rot, value_bf, seg_row, WIN, block_rows)
        attn_flat = attn_out.reshape(TOK_DEV, QW)
        attn_terms = jnp.einsum('tgk,dgk->gtd', widen(attn_out.reshape(TOK_DEV, groups, group_heads * HD)), o_groups)
        attn_sum = lax.optimization_barrier(jnp.sum(round_trip(attn_terms), axis=0))
        attn_normed, attn_unit, attn_inv = rms_forward(attn_sum, post_attn_gain)
        hidden_res = tok_f32 + attn_normed
        normed_mid, unit_mid, inv_mid = rms_forward(hidden_res, pre_ffn_gain)
        normed_mid = normed_mid.astype(jnp.bfloat16)
        gate_pre = jnp.dot(normed_mid, gate_weight, preferred_element_type=jnp.float32)
        up_pre = jnp.dot(normed_mid, up_weight, preferred_element_type=jnp.float32)
        gelu_value, gelu_slope = gelu_parts(gate_pre)
        act_bf = (gelu_value * up_pre).astype(jnp.bfloat16)
        ffn_terms = jnp.einsum('tgk,dgk->gtd', widen(act_bf.reshape(TOK_DEV, groups, group_units)), down_groups)
        ffn_sum = lax.optimization_barrier(jnp.sum(round_trip(ffn_terms), axis=0))
        ffn_normed, ffn_unit, ffn_inv = rms_forward(ffn_sum, post_ffn_gain)
        output = (hidden_res + ffn_normed).astype(jnp.bfloat16)
        grad_out = grad_seq.astype(jnp.float32)
        grad_post_ffn = lax.optimization_barrier(jnp.sum(grad_out * ffn_unit, axis=0))
        grad_ffn_sum = rms_backward(grad_out, ffn_unit, ffn_inv, post_ffn_gain).astype(jnp.bfloat16)
        grad_act = jnp.dot(grad_ffn_sum, down_weight, preferred_element_type=jnp.float32)
        grad_down_w = lax.dot_general(grad_ffn_sum, act_bf, contract_rows, preferred_element_type=jnp.float32)
        grad_gate_bf = (grad_act * up_pre * gelu_slope).astype(jnp.bfloat16)
        grad_up_bf = (grad_act * gelu_value).astype(jnp.bfloat16)
        grad_gate_w = lax.dot_general(normed_mid, grad_gate_bf, contract_rows, preferred_element_type=jnp.float32)
        grad_up_w = lax.dot_general(normed_mid, grad_up_bf, contract_rows, preferred_element_type=jnp.float32)
        grad_mid_groups = jnp.einsum('tgk,dgk->gtd', widen(grad_gate_bf.reshape(TOK_DEV, groups, group_units)), gate_groups)
        grad_mid_groups = grad_mid_groups + jnp.einsum('tgk,dgk->gtd', widen(grad_up_bf.reshape(TOK_DEV, groups, group_units)), up_groups)
        grad_pre_ffn = lax.optimization_barrier(jnp.sum(grad_mid_groups * unit_mid[None], axis=(0, 1)))
        ffn_back = lax.optimization_barrier(jnp.sum(round_trip(rms_backward(grad_mid_groups, unit_mid[None], inv_mid[None], pre_ffn_gain)), axis=0))
        grad_hidden = grad_out + ffn_back
        grad_post_attn = lax.optimization_barrier(jnp.sum(grad_hidden * attn_unit, axis=0))
        grad_attn_sum = rms_backward(grad_hidden, attn_unit, attn_inv, post_attn_gain).astype(jnp.bfloat16)
        grad_attn = jnp.dot(grad_attn_sum, o_weight, preferred_element_type=jnp.float32).astype(jnp.bfloat16).reshape(TOK_DEV, NH, HD)
        grad_o_w = lax.dot_general(grad_attn_sum, attn_flat, contract_rows, preferred_element_type=jnp.float32)
        grad_query, grad_keys, grad_values = attend_backward(query_rot, key_rot, value_bf, attn_out, grad_attn, lse_rows, seg_row, WIN, block_rows)
        grad_qnorm = unrotate(grad_query, cosine, sine_tab)
        grad_query_gain = lax.optimization_barrier(jnp.sum(grad_qnorm * query_unit, axis=(0, 1)))
        grad_query_bf = rms_backward(grad_qnorm, query_unit, query_inv, query_gain).astype(jnp.bfloat16)
        grad_key_groups = lax.optimization_barrier(jnp.sum(grad_keys.reshape(TOK_DEV, groups, group_heads, HD), axis=2))
        grad_knorm = unrotate(grad_key_groups, cosine, sine_tab)
        grad_key_gain = lax.optimization_barrier(jnp.sum(grad_knorm * key_unit[:, None, :], axis=(0, 1)))
        grad_key_bf = rms_backward(grad_knorm, key_unit[:, None, :], key_inv[:, None, :], key_gain).astype(jnp.bfloat16)
        grad_value_bf = lax.optimization_barrier(jnp.sum(grad_values.reshape(TOK_DEV, groups, group_heads, HD), axis=2)).astype(jnp.bfloat16)
        grad_q_w = lax.dot_general(normed_in, grad_query_bf.reshape(TOK_DEV, QW), contract_rows, preferred_element_type=jnp.float32)
        grad_k_w = jnp.einsum('td,tgk->dk', widen(normed_in), widen(grad_key_bf))
        grad_v_w = jnp.einsum('td,tgk->dk', widen(normed_in), widen(grad_value_bf))
        grad_in_groups = jnp.einsum('tgk,dgk->gtd', widen(grad_query_bf.reshape(TOK_DEV, groups, group_heads * HD)), q_groups)
        grad_in_groups = grad_in_groups + jnp.einsum('tgk,dk->gtd', widen(grad_key_bf), k_wide)
        grad_in_groups = grad_in_groups + jnp.einsum('tgk,dk->gtd', widen(grad_value_bf), v_wide)
        grad_input_gain = lax.optimization_barrier(jnp.sum(grad_in_groups * unit_in[None], axis=(0, 1)))
        attn_back = lax.optimization_barrier(jnp.sum(round_trip(rms_backward(grad_in_groups, unit_in[None], inv_in[None], input_gain)), axis=0))
        grad_tokens = grad_hidden + attn_back
        fresh = (grad_input_gain, grad_q_w, grad_k_w, grad_v_w, grad_query_gain, grad_key_gain, grad_o_w, grad_post_attn, grad_pre_ffn, grad_gate_w, grad_up_w, grad_down_w, grad_post_ffn)
        return (jax.tree.map(jnp.add, totals, fresh), (output, grad_tokens))
    init = (jnp.zeros((D,), jnp.float32), jnp.zeros((D, QW), jnp.float32), jnp.zeros((D, HD), jnp.float32), jnp.zeros((D, HD), jnp.float32), jnp.zeros((HD,), jnp.float32), jnp.zeros((HD,), jnp.float32), jnp.zeros((D, QW), jnp.float32), jnp.zeros((D,), jnp.float32), jnp.zeros((D,), jnp.float32), jnp.zeros((D, FF), jnp.float32), jnp.zeros((D, FF), jnp.float32), jnp.zeros((D, FF), jnp.float32), jnp.zeros((D,), jnp.float32))
    inputs = (tokens.reshape(N_DP, TOK_DEV, D), segment_ids, out_grad.reshape(N_DP, TOK_DEV, D))
    totals, (outputs, grad_rows) = lax.scan(one_sequence, init, inputs)
    return (outputs.reshape(TOKENS, D), grad_rows.reshape(TOKENS, D), totals[0], totals[1], totals[2], totals[3], totals[4], totals[5], totals[6], totals[7], totals[8], totals[9], totals[10], totals[11], totals[12])
```

```python
import functools

import jax
import jax.numpy as jnp
from jax import lax
from jax.sharding import PartitionSpec as P

HD = 256
WIN = 512


norm_eps = 1e-06
rope_base = 10000.0
gelu_coef = 0.7978845608028654
cube_coef = 0.044715
masked_value = -1e30
contract_rows = (((0,), (0,)), ((), ()))
contract_cols = (((1,), (1,)), ((), ()))


def rms_forward(values, gain_vec):
    inverse = lax.rsqrt(jnp.mean(values * values, axis=-1, keepdims=True) + norm_eps)
    unit_vals = values * inverse
    return (unit_vals * (1.0 + gain_vec), unit_vals, inverse)


def rms_backward(grad_vals, unit_vals, inverse, gain_vec):
    scaled = grad_vals * (1.0 + gain_vec)
    return inverse * (scaled - unit_vals * jnp.mean(scaled * unit_vals, axis=-1, keepdims=True))


def doc_positions(segment_row):
    row_count = segment_row.shape[0]
    row_index = jnp.arange(row_count, dtype=jnp.int32)
    change = jnp.concatenate([jnp.ones((1,), dtype=jnp.bool_), segment_row[1:] != segment_row[:-1]])
    starts = lax.cummax(jnp.where(change, row_index, 0), axis=0)
    return row_index - starts


def rope_tables(positions, head_dim):
    half_dim = head_dim // 2
    frequency = rope_base ** (-(jnp.arange(half_dim, dtype=jnp.float32) * 2.0 / head_dim))
    angles = positions.astype(jnp.float32)[:, None] * frequency[None, :]
    return (jnp.cos(angles), jnp.sin(angles))


def rotate(values, cosine, sine_tab):
    half_dim = values.shape[-1] // 2
    first_half = values[..., :half_dim]
    second_half = values[..., half_dim:]
    cos_b = cosine[:, None, :]
    sin_b = sine_tab[:, None, :]
    return jnp.concatenate(
        [first_half * cos_b - second_half * sin_b, second_half * cos_b + first_half * sin_b],
        axis=-1,
    )


def unrotate(values, cosine, sine_tab):
    half_dim = values.shape[-1] // 2
    first_half = values[..., :half_dim]
    second_half = values[..., half_dim:]
    cos_b = cosine[:, None, :]
    sin_b = sine_tab[:, None, :]
    return jnp.concatenate(
        [first_half * cos_b + second_half * sin_b, second_half * cos_b - first_half * sin_b],
        axis=-1,
    )


def gelu_parts(gate_pre):
    inner_arg = gelu_coef * (gate_pre + cube_coef * gate_pre * gate_pre * gate_pre)
    tanh_val = jnp.tanh(inner_arg)
    gelu_value = 0.5 * gate_pre * (1.0 + tanh_val)
    gelu_slope = 0.5 * (1.0 + tanh_val) + 0.5 * gate_pre * (
        1.0 - tanh_val * tanh_val
    ) * gelu_coef * (1.0 + 3.0 * cube_coef * gate_pre * gate_pre)
    return (gelu_value, gelu_slope)


def window_mask(query_seg, key_seg, block_rows, window):
    row_ids = jnp.arange(block_rows, dtype=jnp.int32)[:, None]
    col_ids = jnp.arange(block_rows + window, dtype=jnp.int32)[None, :]
    inside = (col_ids > row_ids) & (col_ids <= row_ids + window)
    return inside & (query_seg[:, None] == key_seg[None, :])


def padded_inputs(key_rows, value_rows, segments, window):
    head_dim = key_rows.shape[-1]
    pad_keys = jnp.concatenate([jnp.zeros((window, head_dim), key_rows.dtype), key_rows], axis=0)
    pad_values = jnp.concatenate(
        [jnp.zeros((window, head_dim), value_rows.dtype), value_rows], axis=0
    )
    pad_segments = jnp.concatenate([jnp.full((window,), -1, jnp.int32), segments], axis=0)
    return (pad_keys, pad_values, pad_segments)


def attend_forward(query_rows, key_rows, value_rows, segments, window, block_rows):
    tok_count, head_count, head_dim = query_rows.shape
    score_scale = head_dim ** (-0.5)
    pad_keys, pad_values, pad_segments = padded_inputs(key_rows, value_rows, segments, window)
    key_span = block_rows + window

    def one_block(row_start):
        query_blk = lax.dynamic_slice_in_dim(query_rows, row_start, block_rows, 0)
        key_blk = lax.dynamic_slice_in_dim(pad_keys, row_start, key_span, 0)
        value_blk = lax.dynamic_slice_in_dim(pad_values, row_start, key_span, 0)
        allowed = window_mask(
            lax.dynamic_slice_in_dim(segments, row_start, block_rows, 0),
            lax.dynamic_slice_in_dim(pad_segments, row_start, key_span, 0),
            block_rows,
            window,
        )
        scores = (
            jnp.einsum("bhd,kd->hbk", query_blk, key_blk, preferred_element_type=jnp.float32)
            * score_scale
        )
        row_max = jnp.max(jnp.where(allowed, scores, masked_value), axis=-1, keepdims=True)
        exp_vals = jnp.exp(jnp.where(allowed, scores - row_max, masked_value))
        row_total = jnp.sum(exp_vals, axis=-1, keepdims=True)
        prob_bf = (exp_vals / row_total).astype(jnp.bfloat16)
        result = jnp.einsum(
            "hbk,kd->bhd", prob_bf, value_blk, preferred_element_type=jnp.float32
        ).astype(jnp.bfloat16)
        return (result, (row_max + jnp.log(row_total))[..., 0])

    starts = jnp.arange(tok_count // block_rows, dtype=jnp.int32) * block_rows
    results, lse_blocks = lax.map(one_block, starts)
    return (
        results.reshape(tok_count, head_count, head_dim),
        jnp.transpose(lse_blocks, (1, 0, 2)).reshape(head_count, tok_count),
    )


def attend_backward(
    query_rows, key_rows, value_rows, attn_out, grad_attn, lse_rows, segments, window, block_rows
):
    tok_count, head_count, head_dim = query_rows.shape
    score_scale = head_dim ** (-0.5)
    pad_keys, pad_values, pad_segments = padded_inputs(key_rows, value_rows, segments, window)
    key_span = block_rows + window
    delta_rows = jnp.transpose(
        jnp.sum(grad_attn.astype(jnp.float32) * attn_out.astype(jnp.float32), axis=-1)
    )

    def one_block(carry, row_start):
        grad_keys, grad_values = carry
        query_blk = lax.dynamic_slice_in_dim(query_rows, row_start, block_rows, 0)
        key_blk = lax.dynamic_slice_in_dim(pad_keys, row_start, key_span, 0)
        value_blk = lax.dynamic_slice_in_dim(pad_values, row_start, key_span, 0)
        allowed = window_mask(
            lax.dynamic_slice_in_dim(segments, row_start, block_rows, 0),
            lax.dynamic_slice_in_dim(pad_segments, row_start, key_span, 0),
            block_rows,
            window,
        )
        scores = (
            jnp.einsum("bhd,kd->hbk", query_blk, key_blk, preferred_element_type=jnp.float32)
            * score_scale
        )
        lse_blk = lax.dynamic_slice_in_dim(lse_rows, row_start, block_rows, 1)
        probs = jnp.exp(jnp.where(allowed, scores - lse_blk[..., None], masked_value))
        grad_blk = lax.dynamic_slice_in_dim(grad_attn, row_start, block_rows, 0)
        grad_probs = jnp.einsum(
            "bhd,kd->hbk", grad_blk, value_blk, preferred_element_type=jnp.float32
        )
        delta_blk = lax.dynamic_slice_in_dim(delta_rows, row_start, block_rows, 1)
        grad_scores = (probs * (grad_probs - delta_blk[..., None]) * score_scale).astype(
            jnp.bfloat16
        )
        grad_query = jnp.einsum(
            "hbk,kd->bhd", grad_scores, key_blk, preferred_element_type=jnp.float32
        )
        key_part = jnp.einsum(
            "hbk,bhd->khd", grad_scores, query_blk, preferred_element_type=jnp.float32
        )
        value_part = jnp.einsum(
            "hbk,bhd->khd", probs.astype(jnp.bfloat16), grad_blk, preferred_element_type=jnp.float32
        )
        grad_keys = lax.dynamic_update_slice_in_dim(
            grad_keys,
            lax.dynamic_slice_in_dim(grad_keys, row_start, key_span, 0) + key_part,
            row_start,
            0,
        )
        grad_values = lax.dynamic_update_slice_in_dim(
            grad_values,
            lax.dynamic_slice_in_dim(grad_values, row_start, key_span, 0) + value_part,
            row_start,
            0,
        )
        return ((grad_keys, grad_values), grad_query)

    zeros_init = jnp.zeros((tok_count + window, head_count, head_dim), jnp.float32)
    starts = jnp.arange(tok_count // block_rows, dtype=jnp.int32) * block_rows
    (grad_keys, grad_values), grad_query = lax.scan(one_block, (zeros_init, zeros_init), starts)
    return (
        grad_query.reshape(tok_count, head_count, head_dim),
        grad_keys[window:],
        grad_values[window:],
    )


def flip_pairs(size, bit):
    return [(index, index ^ bit) for index in range(size)]


def sum_tensor(term, size):
    rows = term.shape[0]
    half = rows // 2
    low = lax.rem(lax.axis_index("tensor"), 2)
    term = lax.optimization_barrier(term.astype(jnp.bfloat16))
    mine = lax.dynamic_slice_in_dim(term, low * half, half, 0)
    other = lax.dynamic_slice_in_dim(term, (1 - low) * half, half, 0)
    got = lax.ppermute(other, "tensor", flip_pairs(size, 1))
    total = mine.astype(jnp.float32) + got.astype(jnp.float32)
    bit = 2
    while bit < size:
        sent = lax.optimization_barrier(total.astype(jnp.bfloat16))
        got = lax.ppermute(sent, "tensor", flip_pairs(size, bit))
        total = sent.astype(jnp.float32) + got.astype(jnp.float32)
        bit *= 2
    sent = lax.optimization_barrier(total.astype(jnp.bfloat16))
    got = lax.ppermute(sent, "tensor", flip_pairs(size, 1))
    first = jnp.where(low == 0, sent, got)
    second = jnp.where(low == 0, got, sent)
    return jnp.concatenate([first, second], axis=0).astype(jnp.float32)


def sum_small(values, size):
    total = values
    bit = 1
    while bit < size:
        sent = lax.optimization_barrier(total.astype(jnp.bfloat16))
        got = lax.ppermute(sent, "tensor", flip_pairs(size, bit))
        total = sent.astype(jnp.float32) + got.astype(jnp.float32)
        bit *= 2
    return total


def scatter_dp(blocks, size):
    index = lax.axis_index("dp")
    rows, cols = blocks.shape[1:]
    total = blocks
    bit = 1
    while bit < size:
        low = lax.rem(lax.div(index, bit), 2)
        parts = total.reshape(-1, 2, rows, cols)
        sent = lax.optimization_barrier(
            lax.dynamic_index_in_dim(parts, 1 - low, 1, keepdims=False).astype(jnp.bfloat16)
        )
        kept = lax.dynamic_index_in_dim(parts, low, 1, keepdims=False)
        got = lax.ppermute(sent, "dp", flip_pairs(size, bit))
        total = kept.astype(jnp.float32) + got.astype(jnp.float32)
        bit *= 2
    return total.reshape(rows, cols)


def on_device(
    tensor_size,
    dp_size,
    tokens,
    segment_ids,
    input_gain,
    q_weight,
    k_weight,
    v_weight,
    query_gain,
    key_gain,
    o_weight,
    post_attn_gain,
    pre_ffn_gain,
    gate_weight,
    up_weight,
    down_weight,
    post_ffn_gain,
    out_grad,
):
    tok_count = tokens.shape[0]
    head_local = q_weight.shape[1] // HD
    block_rows = min(512, tok_count)
    segments = segment_ids[0]
    positions = doc_positions(segments)
    cosine, sine_tab = rope_tables(positions, HD)
    tok_f32 = tokens.astype(jnp.float32)
    normed_in, unit_in, inv_in = rms_forward(tok_f32, input_gain)
    normed_in = normed_in.astype(jnp.bfloat16)
    query_raw = jnp.dot(normed_in, q_weight, preferred_element_type=jnp.float32).reshape(
        tok_count, head_local, HD
    )
    key_raw = jnp.dot(normed_in, k_weight, preferred_element_type=jnp.float32)
    value_bf = jnp.dot(normed_in, v_weight, preferred_element_type=jnp.float32).astype(jnp.bfloat16)
    query_normed, query_unit, query_inv = rms_forward(query_raw, query_gain)
    key_normed, key_unit, key_inv = rms_forward(key_raw, key_gain)
    query_rot = rotate(query_normed, cosine, sine_tab).astype(jnp.bfloat16)
    key_rot = rotate(key_normed[:, None, :], cosine, sine_tab)[:, 0, :].astype(jnp.bfloat16)
    attn_out, lse_rows = attend_forward(query_rot, key_rot, value_bf, segments, WIN, block_rows)
    attn_flat = attn_out.reshape(tok_count, head_local * HD)
    attn_term = lax.dot_general(
        attn_flat, o_weight, contract_cols, preferred_element_type=jnp.float32
    )
    attn_sum = sum_tensor(attn_term, tensor_size)
    attn_normed, attn_unit, attn_inv = rms_forward(attn_sum, post_attn_gain)
    hidden_res = tok_f32 + attn_normed
    normed_mid, unit_mid, inv_mid = rms_forward(hidden_res, pre_ffn_gain)
    normed_mid = normed_mid.astype(jnp.bfloat16)
    gate_pre = jnp.dot(normed_mid, gate_weight, preferred_element_type=jnp.float32)
    up_pre = jnp.dot(normed_mid, up_weight, preferred_element_type=jnp.float32)
    gelu_value, gelu_slope = gelu_parts(gate_pre)
    act_bf = (gelu_value * up_pre).astype(jnp.bfloat16)
    ffn_term = lax.dot_general(
        act_bf, down_weight, contract_cols, preferred_element_type=jnp.float32
    )
    ffn_sum = sum_tensor(ffn_term, tensor_size)
    ffn_normed, ffn_unit, ffn_inv = rms_forward(ffn_sum, post_ffn_gain)
    output = (hidden_res + ffn_normed).astype(jnp.bfloat16)
    grad_out = out_grad.astype(jnp.float32)
    grad_post_ffn = jnp.sum(grad_out * ffn_unit, axis=0)
    grad_ffn_sum = rms_backward(grad_out, ffn_unit, ffn_inv, post_ffn_gain).astype(jnp.bfloat16)
    grad_act = jnp.dot(grad_ffn_sum, down_weight, preferred_element_type=jnp.float32)
    grad_down_w = lax.dot_general(
        grad_ffn_sum, act_bf, contract_rows, preferred_element_type=jnp.float32
    )
    grad_gate_bf = (grad_act * up_pre * gelu_slope).astype(jnp.bfloat16)
    grad_up_bf = (grad_act * gelu_value).astype(jnp.bfloat16)
    grad_gate_w = lax.dot_general(
        normed_mid, grad_gate_bf, contract_rows, preferred_element_type=jnp.float32
    )
    grad_up_w = lax.dot_general(
        normed_mid, grad_up_bf, contract_rows, preferred_element_type=jnp.float32
    )
    grad_mid = lax.dot_general(
        grad_gate_bf, gate_weight, contract_cols, preferred_element_type=jnp.float32
    )
    grad_mid = grad_mid + lax.dot_general(
        grad_up_bf, up_weight, contract_cols, preferred_element_type=jnp.float32
    )
    grad_pre_ffn = jnp.sum(grad_mid * unit_mid, axis=0)
    ffn_back = sum_tensor(rms_backward(grad_mid, unit_mid, inv_mid, pre_ffn_gain), tensor_size)
    grad_hidden = grad_out + ffn_back
    grad_post_attn = jnp.sum(grad_hidden * attn_unit, axis=0)
    grad_attn_sum = rms_backward(grad_hidden, attn_unit, attn_inv, post_attn_gain).astype(
        jnp.bfloat16
    )
    grad_attn = (
        jnp.dot(grad_attn_sum, o_weight, preferred_element_type=jnp.float32)
        .astype(jnp.bfloat16)
        .reshape(tok_count, head_local, HD)
    )
    grad_o_w = lax.dot_general(
        grad_attn_sum, attn_flat, contract_rows, preferred_element_type=jnp.float32
    )
    grad_query, grad_keys, grad_values = attend_backward(
        query_rot, key_rot, value_bf, attn_out, grad_attn, lse_rows, segments, WIN, block_rows
    )
    grad_qnorm = unrotate(grad_query, cosine, sine_tab)
    grad_query_gain = jnp.sum(grad_qnorm * query_unit, axis=(0, 1))
    grad_query_bf = (
        rms_backward(grad_qnorm, query_unit, query_inv, query_gain)
        .astype(jnp.bfloat16)
        .reshape(tok_count, head_local * HD)
    )
    grad_knorm = unrotate(jnp.sum(grad_keys, axis=1, keepdims=True), cosine, sine_tab)[:, 0, :]
    grad_key_gain = jnp.sum(grad_knorm * key_unit, axis=0)
    grad_key_bf = rms_backward(grad_knorm, key_unit, key_inv, key_gain).astype(jnp.bfloat16)
    grad_value_bf = jnp.sum(grad_values, axis=1).astype(jnp.bfloat16)
    grad_q_w = lax.dot_general(
        normed_in, grad_query_bf, contract_rows, preferred_element_type=jnp.float32
    )
    grad_k_w = lax.dot_general(
        normed_in, grad_key_bf, contract_rows, preferred_element_type=jnp.float32
    )
    grad_v_w = lax.dot_general(
        normed_in, grad_value_bf, contract_rows, preferred_element_type=jnp.float32
    )
    grad_in = lax.dot_general(
        grad_query_bf, q_weight, contract_cols, preferred_element_type=jnp.float32
    )
    grad_in = grad_in + lax.dot_general(
        grad_key_bf, k_weight, contract_cols, preferred_element_type=jnp.float32
    )
    grad_in = grad_in + lax.dot_general(
        grad_value_bf, v_weight, contract_cols, preferred_element_type=jnp.float32
    )
    grad_input_gain = jnp.sum(grad_in * unit_in, axis=0)
    attn_back = sum_tensor(rms_backward(grad_in, unit_in, inv_in, input_gain), tensor_size)
    grad_tokens = grad_hidden + attn_back
    model, head_dim = grad_k_w.shape
    part_rows = model // dp_size
    early = jnp.concatenate([grad_o_w, grad_gate_w, grad_up_w, grad_down_w], axis=1)
    early = early.astype(jnp.bfloat16).reshape(dp_size, part_rows, -1)
    early = scatter_dp(early, dp_size)
    gains = jnp.concatenate(
        [grad_post_attn, grad_post_ffn, grad_input_gain, grad_pre_ffn, grad_query_gain, grad_key_gain]
    )
    gain_count = gains.shape[0]
    late_cols = grad_q_w.shape[1] + 2 * head_dim
    gain_rows = -(-gain_count // (16 * late_cols)) * 16
    gains = jnp.pad(gains, (0, gain_rows * late_cols - gain_count)).reshape(1, gain_rows, late_cols)
    late = jnp.concatenate([grad_q_w, grad_k_w, grad_v_w], axis=1)
    late = late.reshape(dp_size, part_rows, late_cols)
    late = jnp.concatenate(
        [late, jnp.broadcast_to(gains, (dp_size, gain_rows, late_cols))], axis=1
    ).astype(jnp.bfloat16)
    late = scatter_dp(late, dp_size)
    q_cols = grad_q_w.shape[1]
    grad_q_w = late[:part_rows, :q_cols]
    kv_part = late[:part_rows, q_cols:]
    gain_part = late[part_rows:].reshape(-1)[:gain_count]
    shared = jnp.concatenate([kv_part.reshape(-1), gain_part]).reshape(-1, 128)
    shared = sum_small(shared, tensor_size).reshape(-1)
    kv_sum = shared[: part_rows * 2 * head_dim].reshape(part_rows, 2 * head_dim)
    gain_sum = shared[part_rows * 2 * head_dim :]
    grad_k_w = kv_sum[:, :head_dim]
    grad_v_w = kv_sum[:, head_dim:]
    grad_post_attn = gain_part[:model]
    grad_post_ffn = gain_part[model : 2 * model]
    grad_input_gain = gain_sum[2 * model : 3 * model]
    grad_pre_ffn = gain_sum[3 * model : 4 * model]
    grad_query_gain = gain_sum[4 * model : 4 * model + head_dim]
    grad_key_gain = gain_sum[4 * model + head_dim :]
    widths = (grad_o_w.shape[1], grad_gate_w.shape[1], grad_up_w.shape[1])
    at = 0
    pieces = []
    for width in widths:
        pieces.append(early[:, at : at + width])
        at += width
    grad_o_w, grad_gate_w, grad_up_w = pieces
    grad_down_w = early[:, at:]
    return (
        output,
        grad_tokens,
        grad_input_gain,
        grad_q_w,
        grad_k_w,
        grad_v_w,
        grad_query_gain,
        grad_key_gain,
        grad_o_w,
        grad_post_attn,
        grad_pre_ffn,
        grad_gate_w,
        grad_up_w,
        grad_down_w,
        grad_post_ffn,
    )


def solution(mesh):
    in_specs = (
        P("dp", None),
        P("dp", None),
        P(),
        P(None, "tensor"),
        P(),
        P(),
        P(),
        P(),
        P(None, "tensor"),
        P(),
        P(),
        P(None, "tensor"),
        P(None, "tensor"),
        P(None, "tensor"),
        P(),
        P("dp", None),
    )
    out_specs = (
        P("dp", None),
        P("dp", None),
        P(),
        P("dp", "tensor"),
        P("dp", None),
        P("dp", None),
        P(),
        P(),
        P("dp", "tensor"),
        P(),
        P(),
        P("dp", "tensor"),
        P("dp", "tensor"),
        P("dp", "tensor"),
        P(),
    )
    body = functools.partial(on_device, mesh.shape["tensor"], mesh.shape["dp"])
    return jax.shard_map(
        body, mesh=mesh, in_specs=in_specs, out_specs=out_specs, check_vma=False
    )
```

```python
import functools

import jax
import jax.numpy as jnp
from jax import lax
from jax.experimental import pallas as pl
from jax.experimental.pallas import tpu as pltpu
from jax.sharding import PartitionSpec as P

WIN = 512
ROWS = 256


norm_eps = 1e-06
rope_base = 10000.0
gelu_coef = 0.7978845608028654
cube_coef = 0.044715
masked_value = -1e30
contract_rows = (((0,), (0,)), ((), ()))
contract_cols = (((1,), (1,)), ((), ()))
F32 = jnp.float32
BF16 = jnp.bfloat16


def mat(left, right):
    return jnp.dot(left, right, preferred_element_type=F32)


def mat_rows(left, right):
    return lax.dot_general(left, right, contract_rows, preferred_element_type=F32)


def mat_cols(left, right):
    return lax.dot_general(left, right, contract_cols, preferred_element_type=F32)


def rms_unit(values):
    inverse = lax.rsqrt(jnp.mean(values * values, axis=-1, keepdims=True) + norm_eps)
    return (values * inverse, inverse)


def rms_backward(grad_vals, unit_vals, inverse, gain_vec):
    scaled = grad_vals * (1.0 + gain_vec)
    return inverse * (scaled - unit_vals * jnp.mean(scaled * unit_vals, axis=-1, keepdims=True))


def rotate(values, cosine, sine_tab, sign):
    half_dim = values.shape[-1] // 2
    first = values[:, :half_dim]
    second = values[:, half_dim:]
    return jnp.concatenate(
        [first * cosine - sign * second * sine_tab, second * cosine + sign * first * sine_tab],
        axis=-1,
    )


def column_sum(values):
    return jnp.sum(values, axis=0, keepdims=True)


def allowed_keys(low_col, block):
    rows = low_col.shape[0]
    col_ids = lax.broadcasted_iota(jnp.int32, (rows, rows + WIN), 1) - WIN
    row_ids = lax.broadcasted_iota(jnp.int32, (rows, rows + WIN), 0)
    return (col_ids >= low_col - block * rows) & (col_ids <= row_ids)


def attend_kernel(
    tok, gain, q_w, k_w, v_w, q_gain, k_gain, o_w, cosine, sine_tab, low,
    term, attn, q_rot, k_pad, v_pad, stats, q_unit, k_unit,
):
    block = pl.program_id(0)
    rows, head_dim = attn.shape

    @pl.when(block == 0)
    def _():
        k_pad[:WIN, :] = jnp.zeros((WIN, head_dim), BF16)
        v_pad[:WIN, :] = jnp.zeros((WIN, head_dim), BF16)

    unit_in, _ = rms_unit(tok[...].astype(F32))
    normed = (unit_in * (1.0 + gain[...])).astype(BF16)
    cos_b, sin_b = cosine[...], sine_tab[...]
    q_u, q_inv = rms_unit(mat(normed, q_w[...]))
    k_u, k_inv = rms_unit(mat(normed, k_w[...]))
    q_unit[...] = q_u
    k_unit[...] = k_u
    q_r = rotate(q_u * (1.0 + q_gain[...]), cos_b, sin_b, 1.0).astype(BF16)
    q_rot[...] = q_r
    here = pl.ds(pl.multiple_of(block * rows + WIN, rows), rows)
    span = pl.ds(pl.multiple_of(block * rows, rows), rows + WIN)
    k_pad[here, :] = rotate(k_u * (1.0 + k_gain[...]), cos_b, sin_b, 1.0).astype(BF16)
    v_pad[here, :] = mat(normed, v_w[...]).astype(BF16)
    scores = mat_cols(q_r, k_pad[span, :]) * (head_dim ** (-0.5))
    scores = jnp.where(allowed_keys(low[...], block), scores, masked_value)
    row_max = jnp.max(scores, axis=-1, keepdims=True)
    exp_vals = jnp.exp(scores - row_max)
    row_total = jnp.sum(exp_vals, axis=-1, keepdims=True)
    probs = (exp_vals * (1.0 / row_total)).astype(BF16)
    result = mat(probs, v_pad[span, :]).astype(BF16)
    attn[...] = result
    term[...] = mat_cols(result, o_w[...]).astype(BF16)
    lane = lax.broadcasted_iota(jnp.int32, stats.shape, 1)
    lse = row_max + jnp.log(row_total)
    stats[...] = jnp.where(lane == 0, lse, jnp.where(lane == 1, q_inv, k_inv))


def middle(tok, attn_sum, post_attn_gain):
    attn_unit, attn_inv = rms_unit(attn_sum[...].astype(F32))
    hidden = tok[...].astype(F32) + attn_unit * (1.0 + post_attn_gain[...])
    mid_unit, mid_inv = rms_unit(hidden)
    return (attn_unit, attn_inv, hidden, mid_unit, mid_inv)


def ffn_kernel(tok, attn_sum, pa_gain, pre_gain, gate_w, up_w, down_w, term, gate, up):
    _, _, _, mid_unit, _ = middle(tok, attn_sum, pa_gain)
    normed = (mid_unit * (1.0 + pre_gain[...])).astype(BF16)
    gate_pre = mat(normed, gate_w[...])
    up_pre = mat(normed, up_w[...])
    gate[...] = gate_pre
    up[...] = up_pre
    tanh_val = jnp.tanh(gelu_coef * (gate_pre + cube_coef * gate_pre * gate_pre * gate_pre))
    act = (0.5 * gate_pre * (1.0 + tanh_val) * up_pre).astype(BF16)
    term[...] = mat_cols(act, down_w[...]).astype(BF16)


def ffn_back_kernel(
    tok, attn_sum, ffn_sum, out_grad, gate, up, pa_gain, pre_gain, pf_gain, gate_w, up_w, down_w,
    output, term, weight_grads, gains, total,
):
    block = pl.program_id(0)

    @pl.when(block == 0)
    def _():
        total[...] = jnp.zeros_like(total)
        gains[...] = jnp.zeros_like(gains)

    _, _, hidden, mid_unit, mid_inv = middle(tok, attn_sum, pa_gain)
    normed = (mid_unit * (1.0 + pre_gain[...])).astype(BF16)
    ffn_unit, ffn_inv = rms_unit(ffn_sum[...].astype(F32))
    output[...] = (hidden + ffn_unit * (1.0 + pf_gain[...])).astype(BF16)
    grad_out = out_grad[...].astype(F32)
    gains[0:1, :] += column_sum(grad_out * ffn_unit)
    grad_sum = rms_backward(grad_out, ffn_unit, ffn_inv, pf_gain[...]).astype(BF16)
    grad_act = mat(grad_sum, down_w[...])
    gate_pre, up_pre = gate[...], up[...]
    squared = gate_pre * gate_pre
    tanh_val = jnp.tanh(gelu_coef * (gate_pre + cube_coef * squared * gate_pre))
    gelu_value = 0.5 * gate_pre * (1.0 + tanh_val)
    slope = 0.5 * (1.0 + tanh_val) + 0.5 * gate_pre * (1.0 - tanh_val * tanh_val) * gelu_coef * (
        1.0 + 3.0 * cube_coef * squared
    )
    act = (gelu_value * up_pre).astype(BF16)
    grad_gate = (grad_act * up_pre * slope).astype(BF16)
    grad_up = (grad_act * gelu_value).astype(BF16)
    units = gate_pre.shape[1]
    total[:, :units] += mat_rows(normed, grad_gate)
    total[:, units : 2 * units] += mat_rows(normed, grad_up)
    total[:, 2 * units :] += mat_rows(grad_sum, act)
    grad_mid = mat_cols(grad_gate, gate_w[...]) + mat_cols(grad_up, up_w[...])
    gains[1:2, :] += column_sum(grad_mid * mid_unit)
    term[...] = rms_backward(grad_mid, mid_unit, mid_inv, pre_gain[...]).astype(BF16)

    @pl.when(block == pl.num_programs(0) - 1)
    def _():
        weight_grads[...] = total[...].astype(BF16)


def attend_back_kernel(
    tok, out_grad, ffn_back, attn_sum, attn, q_rot, stats, q_unit, k_unit, cosine, sine_tab, low,
    k_pad, v_pad, pa_gain, in_gain, q_gain, k_gain, q_w, k_w, v_w, o_w,
    term, weight_grads, gains, head_gains, total, grad_k, grad_v,
):
    step = pl.program_id(0)
    block = pl.num_programs(0) - 1 - step
    rows, head_dim = attn.shape
    scale = head_dim ** (-0.5)

    @pl.when(step == 0)
    def _():
        for ref in (total, gains, head_gains, grad_k, grad_v):
            ref[...] = jnp.zeros_like(ref)

    attn_unit, attn_inv = rms_unit(attn_sum[...].astype(F32))
    grad_hidden = out_grad[...].astype(F32) + ffn_back[...].astype(F32)
    gains[0:1, :] += column_sum(grad_hidden * attn_unit)
    grad_sum = rms_backward(grad_hidden, attn_unit, attn_inv, pa_gain[...]).astype(BF16)
    grad_attn = mat(grad_sum, o_w[...]).astype(BF16)
    attn_vals = attn[...]
    total[:, :head_dim] += mat_rows(grad_sum, attn_vals)
    delta = jnp.sum(grad_attn.astype(F32) * attn_vals.astype(F32), axis=-1, keepdims=True)
    span = pl.ds(pl.multiple_of(block * rows, rows), rows + WIN)
    here = pl.ds(pl.multiple_of(block * rows + WIN, rows), rows)
    q_r = q_rot[...]
    k_span, v_span = k_pad[span, :], v_pad[span, :]
    scores = mat_cols(q_r, k_span) * scale
    allowed = allowed_keys(low[...], block)
    probs = jnp.exp(jnp.where(allowed, scores - stats[:, 0:1], masked_value))
    grad_probs = mat_cols(grad_attn, v_span)
    grad_scores = (probs * (grad_probs - delta) * scale).astype(BF16)
    grad_query = mat(grad_scores, k_span)
    grad_k[span, :] += mat_rows(grad_scores, q_r)
    grad_v[span, :] += mat_rows(probs.astype(BF16), grad_attn)
    cos_b, sin_b = cosine[...], sine_tab[...]
    grad_q_unit = rotate(grad_query, cos_b, sin_b, -1.0)
    grad_k_unit = rotate(grad_k[here, :], cos_b, sin_b, -1.0)
    q_u, k_u = q_unit[...], k_unit[...]
    head_gains[0:1, :] += column_sum(grad_q_unit * q_u)
    head_gains[1:2, :] += column_sum(grad_k_unit * k_u)
    grad_q_bf = rms_backward(grad_q_unit, q_u, stats[:, 1:2], q_gain[...]).astype(BF16)
    grad_k_bf = rms_backward(grad_k_unit, k_u, stats[:, 2:3], k_gain[...]).astype(BF16)
    grad_v_bf = grad_v[here, :].astype(BF16)
    unit_in, inv_in = rms_unit(tok[...].astype(F32))
    normed = (unit_in * (1.0 + in_gain[...])).astype(BF16)
    total[:, head_dim : 2 * head_dim] += mat_rows(normed, grad_q_bf)
    total[:, 2 * head_dim : 3 * head_dim] += mat_rows(normed, grad_k_bf)
    total[:, 3 * head_dim :] += mat_rows(normed, grad_v_bf)
    grad_in = mat_cols(grad_q_bf, q_w[...]) + mat_cols(grad_k_bf, k_w[...])
    grad_in = grad_in + mat_cols(grad_v_bf, v_w[...])
    gains[1:2, :] += column_sum(grad_in * unit_in)
    term[...] = rms_backward(grad_in, unit_in, inv_in, in_gain[...]).astype(BF16)

    @pl.when(block == 0)
    def _():
        weight_grads[...] = total[...].astype(BF16)


def row_call(kernel, name, steps, row_args, full_args, row_outs, full_outs, scratch, flops, reverse):
    def row_map(i):
        return (steps - 1 - i if reverse else i, 0)

    def full_map(i):
        return (0, 0)

    def row_spec(shape):
        return pl.BlockSpec((shape[0] // steps, shape[1]), row_map)

    def full_spec(shape):
        return pl.BlockSpec(shape, full_map)

    moved = sum(x.size * x.dtype.itemsize for x in tuple(row_args) + tuple(full_args))
    return pl.pallas_call(
        kernel,
        name=name,
        out_shape=tuple(jax.ShapeDtypeStruct(s, d) for s, d in tuple(row_outs) + tuple(full_outs)),
        grid_spec=pltpu.PrefetchScalarGridSpec(
            num_scalar_prefetch=0,
            grid=(steps,),
            in_specs=[row_spec(x.shape) for x in row_args] + [full_spec(x.shape) for x in full_args],
            out_specs=[row_spec(s) for s, _ in row_outs] + [full_spec(s) for s, _ in full_outs],
            scratch_shapes=scratch,
        ),
        compiler_params=pltpu.CompilerParams(
            dimension_semantics=("arbitrary",), vmem_limit_bytes=48 * 1024 * 1024
        ),
        cost_estimate=pl.CostEstimate(flops=flops, bytes_accessed=moved, transcendentals=0),
    )(*row_args, *full_args)


def flip_pairs(size, bit):
    return [(index, index ^ bit) for index in range(size)]


def sum_tensor(term, size):
    rows = term.shape[0]
    half = rows // 2
    low = lax.rem(lax.axis_index("tensor"), 2)
    term = lax.optimization_barrier(term.astype(jnp.bfloat16))
    mine = lax.dynamic_slice_in_dim(term, low * half, half, 0)
    other = lax.dynamic_slice_in_dim(term, (1 - low) * half, half, 0)
    got = lax.ppermute(other, "tensor", flip_pairs(size, 1))
    total = mine.astype(jnp.float32) + got.astype(jnp.float32)
    bit = 2
    while bit < size:
        sent = lax.optimization_barrier(total.astype(jnp.bfloat16))
        got = lax.ppermute(sent, "tensor", flip_pairs(size, bit))
        total = sent.astype(jnp.float32) + got.astype(jnp.float32)
        bit *= 2
    sent = lax.optimization_barrier(total.astype(jnp.bfloat16))
    got = lax.ppermute(sent, "tensor", flip_pairs(size, 1))
    first = jnp.where(low == 0, sent, got)
    second = jnp.where(low == 0, got, sent)
    return jnp.concatenate([first, second], axis=0)


def sum_small(values, size):
    total = values
    bit = 1
    while bit < size:
        sent = lax.optimization_barrier(total.astype(jnp.bfloat16))
        got = lax.ppermute(sent, "tensor", flip_pairs(size, bit))
        total = sent.astype(jnp.float32) + got.astype(jnp.float32)
        bit *= 2
    return total


def scatter_dp(blocks, size):
    index = lax.axis_index("dp")
    rows, cols = blocks.shape[1:]
    total = blocks
    bit = 1
    while bit < size:
        low = lax.rem(lax.div(index, bit), 2)
        parts = total.reshape(-1, 2, rows, cols)
        sent = lax.optimization_barrier(
            lax.dynamic_index_in_dim(parts, 1 - low, 1, keepdims=False).astype(jnp.bfloat16)
        )
        kept = lax.dynamic_index_in_dim(parts, low, 1, keepdims=False)
        got = lax.ppermute(sent, "dp", flip_pairs(size, bit))
        total = kept.astype(jnp.float32) + got.astype(jnp.float32)
        bit *= 2
    return total.reshape(rows, cols)


def on_device(
    tensor_size,
    dp_size,
    tokens,
    segment_ids,
    input_gain,
    q_weight,
    k_weight,
    v_weight,
    query_gain,
    key_gain,
    o_weight,
    post_attn_gain,
    pre_ffn_gain,
    gate_weight,
    up_weight,
    down_weight,
    post_ffn_gain,
    out_grad,
):
    tok_count, model = tokens.shape
    head_dim = k_weight.shape[1]
    units = gate_weight.shape[1]
    steps = tok_count // ROWS
    segments = segment_ids[0]
    row_index = jnp.arange(tok_count, dtype=jnp.int32)
    starts = jnp.sum((segments[None, :] < segments[:, None]).astype(jnp.int32), axis=1, keepdims=True)
    positions = row_index[:, None] - starts
    low = jnp.maximum(starts, row_index[:, None] - (WIN - 1))
    frequency = rope_base ** (-(jnp.arange(head_dim // 2, dtype=F32) * 2.0 / head_dim))
    angles = positions.astype(F32) * frequency[None, :]
    cosine, sine_tab = jnp.cos(angles), jnp.sin(angles)
    in_gain, pa_gain, pre_gain, pf_gain, q_gain, k_gain = (
        g[None, :]
        for g in (input_gain, post_attn_gain, pre_ffn_gain, post_ffn_gain, query_gain, key_gain)
    )
    square = tok_count * model * head_dim
    attend_full = (in_gain, q_weight, k_weight, v_weight, q_gain, k_gain, o_weight)
    wide = (tok_count, model)
    heads = (tok_count, head_dim)
    padded = (tok_count + WIN, head_dim)

    def attend(tok, cos_b, sin_b, low_b, gain, q_w, k_w, v_w, qg, kg, o_w,
               term, attn, q_rot, stats, q_unit, k_unit, k_pad, v_pad):
        attend_kernel(tok, gain, q_w, k_w, v_w, qg, kg, o_w, cos_b, sin_b, low_b,
                      term, attn, q_rot, k_pad, v_pad, stats, q_unit, k_unit)

    term, attn, q_rot, stats, q_unit, k_unit, k_pad, v_pad = row_call(
        attend, "attend", steps, (tokens, cosine, sine_tab, low), attend_full,
        ((wide, BF16), (heads, BF16), (heads, BF16), ((tok_count, 128), F32), (heads, F32), (heads, F32)),
        ((padded, BF16), (padded, BF16)), (), 14 * square, False,
    )
    attn_sum = sum_tensor(term, tensor_size)
    hidden_shape = (tok_count, units)
    term, gate, up = row_call(
        ffn_kernel, "ffn", steps, (tokens, attn_sum),
        (pa_gain, pre_gain, gate_weight, up_weight, down_weight),
        ((wide, BF16), (hidden_shape, F32), (hidden_shape, F32)), (), (), 12 * square, False,
    )
    ffn_sum = sum_tensor(term, tensor_size)
    output, term, early, ffn_gains = row_call(
        ffn_back_kernel, "ffn_back", steps, (tokens, attn_sum, ffn_sum, out_grad, gate, up),
        (pa_gain, pre_gain, pf_gain, gate_weight, up_weight, down_weight),
        ((wide, BF16), (wide, BF16)), (((model, 3 * units), BF16), ((8, model), F32)),
        (pltpu.VMEM((model, 3 * units), F32),), 24 * square, False,
    )
    part_rows = model // dp_size
    early = scatter_dp(early.reshape(dp_size, part_rows, 3 * units), dp_size)
    ffn_back = sum_tensor(term, tensor_size)
    term, late, attn_gains, head_gains = row_call(
        attend_back_kernel, "attend_back", steps,
        (tokens, out_grad, ffn_back, attn_sum, attn, q_rot, stats, q_unit, k_unit, cosine, sine_tab, low),
        (k_pad, v_pad, pa_gain, in_gain, q_gain, k_gain, q_weight, k_weight, v_weight, o_weight),
        ((wide, BF16),), (((model, 4 * head_dim), BF16), ((8, model), F32), ((8, head_dim), F32)),
        (pltpu.VMEM((model, 4 * head_dim), F32), pltpu.VMEM(padded, F32), pltpu.VMEM(padded, F32)),
        30 * square, True,
    )
    attn_back = sum_tensor(term, tensor_size)
    grad_tokens = out_grad.astype(F32) + ffn_back.astype(F32) + attn_back.astype(F32)
    gains = jnp.concatenate(
        [attn_gains[0], ffn_gains[0], attn_gains[1], ffn_gains[1], head_gains[0], head_gains[1]]
    )
    gain_count = gains.shape[0]
    late_cols = 4 * head_dim
    gain_rows = -(-gain_count // (16 * late_cols)) * 16
    gains = jnp.pad(gains, (0, gain_rows * late_cols - gain_count)).reshape(1, gain_rows, late_cols)
    gains = jnp.broadcast_to(gains.astype(BF16), (dp_size, gain_rows, late_cols))
    late = jnp.concatenate([late.reshape(dp_size, part_rows, late_cols), gains], axis=1)
    late = scatter_dp(late, dp_size)
    grad_o_w = late[:part_rows, :head_dim]
    grad_q_w = late[:part_rows, head_dim : 2 * head_dim]
    gain_part = late[part_rows:].reshape(-1)[:gain_count]
    shared = jnp.concatenate(
        [late[:part_rows, 2 * head_dim :], late[part_rows:].reshape(2 * gain_rows, 2 * head_dim)], axis=0
    )
    shared = sum_small(shared, tensor_size)
    grad_k_w = shared[:part_rows, :head_dim]
    grad_v_w = shared[:part_rows, head_dim:]
    gain_sum = shared[part_rows:].reshape(-1)
    grad_post_attn = gain_part[:model]
    grad_post_ffn = gain_part[model : 2 * model]
    grad_input_gain = gain_sum[2 * model : 3 * model]
    grad_pre_ffn = gain_sum[3 * model : 4 * model]
    grad_query_gain = gain_sum[4 * model : 4 * model + head_dim]
    grad_key_gain = gain_sum[4 * model + head_dim : gain_count]
    grad_gate_w = early[:, :units]
    grad_up_w = early[:, units : 2 * units]
    grad_down_w = early[:, 2 * units :]
    return (
        output, grad_tokens, grad_input_gain, grad_q_w, grad_k_w, grad_v_w, grad_query_gain,
        grad_key_gain, grad_o_w, grad_post_attn, grad_pre_ffn, grad_gate_w, grad_up_w, grad_down_w,
        grad_post_ffn,
    )


def solution(mesh):
    in_specs = (
        P("dp", None),
        P("dp", None),
        P(),
        P(None, "tensor"),
        P(),
        P(),
        P(),
        P(),
        P(None, "tensor"),
        P(),
        P(),
        P(None, "tensor"),
        P(None, "tensor"),
        P(None, "tensor"),
        P(),
        P("dp", None),
    )
    out_specs = (
        P("dp", None),
        P("dp", None),
        P(),
        P("dp", "tensor"),
        P("dp", None),
        P("dp", None),
        P(),
        P(),
        P("dp", "tensor"),
        P(),
        P(),
        P("dp", "tensor"),
        P("dp", "tensor"),
        P("dp", "tensor"),
        P(),
    )
    body = functools.partial(on_device, mesh.shape["tensor"], mesh.shape["dp"])
    return jax.shard_map(
        body, mesh=mesh, in_specs=in_specs, out_specs=out_specs, check_vma=False
    )
```

```python
import functools

import jax
import jax.numpy as jnp
from jax import lax
from jax.experimental import pallas as pl
from jax.experimental.pallas import tpu as pltpu
from jax.sharding import PartitionSpec as P

WIN = 512
ROWS = 256


norm_eps = 1e-06
rope_base = 10000.0
gelu_coef = 0.7978845608028654
cube_coef = 0.044715
masked_value = -1e30
contract_rows = (((0,), (0,)), ((), ()))
contract_cols = (((1,), (1,)), ((), ()))
F32 = jnp.float32
BF16 = jnp.bfloat16


def mat(left, right):
    return jnp.dot(left, right, preferred_element_type=F32)


def mat_rows(left, right):
    return lax.dot_general(left, right, contract_rows, preferred_element_type=F32)


def mat_cols(left, right):
    return lax.dot_general(left, right, contract_cols, preferred_element_type=F32)


def rms_unit(values):
    inverse = lax.rsqrt(jnp.mean(values * values, axis=-1, keepdims=True) + norm_eps)
    return (values * inverse, inverse)


def rms_backward(grad_vals, unit_vals, inverse, gain_vec):
    scaled = grad_vals * (1.0 + gain_vec)
    return inverse * (scaled - unit_vals * jnp.mean(scaled * unit_vals, axis=-1, keepdims=True))


def rotate(values, cosine, sine_tab, sign):
    half_dim = values.shape[-1] // 2
    first = values[:, :half_dim]
    second = values[:, half_dim:]
    return jnp.concatenate(
        [first * cosine - sign * second * sine_tab, second * cosine + sign * first * sine_tab],
        axis=-1,
    )


def column_sum(values):
    return jnp.sum(values, axis=0, keepdims=True)


def allowed_keys(low_col, block):
    rows = low_col.shape[0]
    col_ids = lax.broadcasted_iota(jnp.int32, (rows, rows + WIN), 1) - WIN
    row_ids = lax.broadcasted_iota(jnp.int32, (rows, rows + WIN), 0)
    return (col_ids >= low_col - block * rows) & (col_ids <= row_ids)


def attend_kernel(
    tok, gain, q_w, k_w, v_w, q_gain, k_gain, o_w, cosine, sine_tab, low,
    term, attn, q_rot, k_pad, v_pad, stats, q_unit, k_unit,
):
    block = pl.program_id(0)
    rows, head_dim = attn.shape

    @pl.when(block == 0)
    def _():
        k_pad[:WIN, :] = jnp.zeros((WIN, head_dim), BF16)
        v_pad[:WIN, :] = jnp.zeros((WIN, head_dim), BF16)

    unit_in, _ = rms_unit(tok[...].astype(F32))
    normed = (unit_in * (1.0 + gain[...])).astype(BF16)
    cos_b, sin_b = cosine[...], sine_tab[...]
    q_u, q_inv = rms_unit(mat(normed, q_w[...]))
    k_u, k_inv = rms_unit(mat(normed, k_w[...]))
    q_unit[...] = q_u
    k_unit[...] = k_u
    q_r = rotate(q_u * (1.0 + q_gain[...]), cos_b, sin_b, 1.0).astype(BF16)
    q_rot[...] = q_r
    here = pl.ds(pl.multiple_of(block * rows + WIN, rows), rows)
    span = pl.ds(pl.multiple_of(block * rows, rows), rows + WIN)
    k_pad[here, :] = rotate(k_u * (1.0 + k_gain[...]), cos_b, sin_b, 1.0).astype(BF16)
    v_pad[here, :] = mat(normed, v_w[...]).astype(BF16)
    scores = mat_cols(q_r, k_pad[span, :]) * (head_dim ** (-0.5))
    scores = jnp.where(allowed_keys(low[...], block), scores, masked_value)
    row_max = jnp.max(scores, axis=-1, keepdims=True)
    exp_vals = jnp.exp(scores - row_max)
    row_total = jnp.sum(exp_vals, axis=-1, keepdims=True)
    probs = (exp_vals * (1.0 / row_total)).astype(BF16)
    result = mat(probs, v_pad[span, :]).astype(BF16)
    attn[...] = result
    term[...] = mat_cols(result, o_w[...]).astype(BF16)
    lane = lax.broadcasted_iota(jnp.int32, stats.shape, 1)
    lse = row_max + jnp.log(row_total)
    stats[...] = jnp.where(lane == 0, lse, jnp.where(lane == 1, q_inv, k_inv))


def middle(tok, attn_sum, post_attn_gain):
    attn_unit, attn_inv = rms_unit(attn_sum[...].astype(F32))
    hidden = tok[...].astype(F32) + attn_unit * (1.0 + post_attn_gain[...])
    mid_unit, mid_inv = rms_unit(hidden)
    return (attn_unit, attn_inv, hidden, mid_unit, mid_inv)


def ffn_kernel(tok, attn_sum, pa_gain, pre_gain, gate_w, up_w, down_w, term, gate, up):
    _, _, _, mid_unit, _ = middle(tok, attn_sum, pa_gain)
    normed = (mid_unit * (1.0 + pre_gain[...])).astype(BF16)
    gate_pre = mat(normed, gate_w[...])
    up_pre = mat(normed, up_w[...])
    gate[...] = gate_pre
    up[...] = up_pre
    tanh_val = jnp.tanh(gelu_coef * (gate_pre + cube_coef * gate_pre * gate_pre * gate_pre))
    act = (0.5 * gate_pre * (1.0 + tanh_val) * up_pre).astype(BF16)
    term[...] = mat_cols(act, down_w[...]).astype(BF16)


def ffn_back_kernel(
    tok, attn_sum, ffn_sum, out_grad, gate, up, pa_gain, pre_gain, pf_gain, gate_w, up_w, down_w,
    output, term, weight_grads, gains, total,
):
    block = pl.program_id(0)

    @pl.when(block == 0)
    def _():
        total[...] = jnp.zeros_like(total)
        gains[...] = jnp.zeros_like(gains)

    _, _, hidden, mid_unit, mid_inv = middle(tok, attn_sum, pa_gain)
    normed = (mid_unit * (1.0 + pre_gain[...])).astype(BF16)
    ffn_unit, ffn_inv = rms_unit(ffn_sum[...].astype(F32))
    output[...] = (hidden + ffn_unit * (1.0 + pf_gain[...])).astype(BF16)
    grad_out = out_grad[...].astype(F32)
    gains[0:1, :] += column_sum(grad_out * ffn_unit)
    grad_sum = rms_backward(grad_out, ffn_unit, ffn_inv, pf_gain[...]).astype(BF16)
    grad_act = mat(grad_sum, down_w[...])
    gate_pre, up_pre = gate[...], up[...]
    squared = gate_pre * gate_pre
    tanh_val = jnp.tanh(gelu_coef * (gate_pre + cube_coef * squared * gate_pre))
    gelu_value = 0.5 * gate_pre * (1.0 + tanh_val)
    slope = 0.5 * (1.0 + tanh_val) + 0.5 * gate_pre * (1.0 - tanh_val * tanh_val) * gelu_coef * (
        1.0 + 3.0 * cube_coef * squared
    )
    act = (gelu_value * up_pre).astype(BF16)
    grad_gate = (grad_act * up_pre * slope).astype(BF16)
    grad_up = (grad_act * gelu_value).astype(BF16)
    units = gate_pre.shape[1]
    total[:, :units] += mat_rows(normed, grad_gate)
    total[:, units : 2 * units] += mat_rows(normed, grad_up)
    total[:, 2 * units :] += mat_rows(grad_sum, act)
    grad_mid = mat_cols(grad_gate, gate_w[...]) + mat_cols(grad_up, up_w[...])
    gains[1:2, :] += column_sum(grad_mid * mid_unit)
    term[...] = rms_backward(grad_mid, mid_unit, mid_inv, pre_gain[...]).astype(BF16)

    @pl.when(block == pl.num_programs(0) - 1)
    def _():
        weight_grads[...] = total[...].astype(BF16)


def attend_back_kernel(
    tok, out_grad, ffn_back, attn_sum, attn, q_rot, stats, q_unit, k_unit, cosine, sine_tab, low,
    k_pad, v_pad, pa_gain, in_gain, q_gain, k_gain, q_w, k_w, v_w, o_w,
    term, weight_grads, gains, head_gains, total, grad_k, grad_v,
):
    step = pl.program_id(0)
    block = pl.num_programs(0) - 1 - step
    rows, head_dim = attn.shape
    scale = head_dim ** (-0.5)

    @pl.when(step == 0)
    def _():
        for ref in (total, gains, head_gains, grad_k, grad_v):
            ref[...] = jnp.zeros_like(ref)

    attn_unit, attn_inv = rms_unit(attn_sum[...].astype(F32))
    grad_hidden = out_grad[...].astype(F32) + ffn_back[...].astype(F32)
    gains[0:1, :] += column_sum(grad_hidden * attn_unit)
    grad_sum = rms_backward(grad_hidden, attn_unit, attn_inv, pa_gain[...]).astype(BF16)
    grad_attn = mat(grad_sum, o_w[...]).astype(BF16)
    attn_vals = attn[...]
    total[:, :head_dim] += mat_rows(grad_sum, attn_vals)
    delta = jnp.sum(grad_attn.astype(F32) * attn_vals.astype(F32), axis=-1, keepdims=True)
    span = pl.ds(pl.multiple_of(block * rows, rows), rows + WIN)
    here = pl.ds(pl.multiple_of(block * rows + WIN, rows), rows)
    q_r = q_rot[...]
    k_span, v_span = k_pad[span, :], v_pad[span, :]
    scores = mat_cols(q_r, k_span) * scale
    allowed = allowed_keys(low[...], block)
    probs = jnp.exp(jnp.where(allowed, scores - stats[:, 0:1], masked_value))
    grad_probs = mat_cols(grad_attn, v_span)
    grad_scores = (probs * (grad_probs - delta) * scale).astype(BF16)
    grad_query = mat(grad_scores, k_span)
    grad_k[span, :] += mat_rows(grad_scores, q_r)
    grad_v[span, :] += mat_rows(probs.astype(BF16), grad_attn)
    cos_b, sin_b = cosine[...], sine_tab[...]
    grad_q_unit = rotate(grad_query, cos_b, sin_b, -1.0)
    grad_k_unit = rotate(grad_k[here, :], cos_b, sin_b, -1.0)
    q_u, k_u = q_unit[...], k_unit[...]
    head_gains[0:1, :] += column_sum(grad_q_unit * q_u)
    head_gains[1:2, :] += column_sum(grad_k_unit * k_u)
    grad_q_bf = rms_backward(grad_q_unit, q_u, stats[:, 1:2], q_gain[...]).astype(BF16)
    grad_k_bf = rms_backward(grad_k_unit, k_u, stats[:, 2:3], k_gain[...]).astype(BF16)
    grad_v_bf = grad_v[here, :].astype(BF16)
    unit_in, inv_in = rms_unit(tok[...].astype(F32))
    normed = (unit_in * (1.0 + in_gain[...])).astype(BF16)
    total[:, head_dim : 2 * head_dim] += mat_rows(normed, grad_q_bf)
    total[:, 2 * head_dim : 3 * head_dim] += mat_rows(normed, grad_k_bf)
    total[:, 3 * head_dim :] += mat_rows(normed, grad_v_bf)
    grad_in = mat_cols(grad_q_bf, q_w[...]) + mat_cols(grad_k_bf, k_w[...])
    grad_in = grad_in + mat_cols(grad_v_bf, v_w[...])
    gains[1:2, :] += column_sum(grad_in * unit_in)
    term[...] = rms_backward(grad_in, unit_in, inv_in, in_gain[...]).astype(BF16)

    @pl.when(block == 0)
    def _():
        weight_grads[...] = total[...].astype(BF16)


def row_call(kernel, name, steps, row_args, full_args, row_outs, full_outs, scratch, flops, reverse):
    def row_map(i):
        return (steps - 1 - i if reverse else i, 0)

    def full_map(i):
        return (0, 0)

    def row_spec(shape):
        return pl.BlockSpec((shape[0] // steps, shape[1]), row_map)

    def full_spec(shape):
        return pl.BlockSpec(shape, full_map)

    moved = sum(x.size * x.dtype.itemsize for x in tuple(row_args) + tuple(full_args))
    return pl.pallas_call(
        kernel,
        name=name,
        out_shape=tuple(jax.ShapeDtypeStruct(s, d) for s, d in tuple(row_outs) + tuple(full_outs)),
        grid_spec=pltpu.PrefetchScalarGridSpec(
            num_scalar_prefetch=0,
            grid=(steps,),
            in_specs=[row_spec(x.shape) for x in row_args] + [full_spec(x.shape) for x in full_args],
            out_specs=[row_spec(s) for s, _ in row_outs] + [full_spec(s) for s, _ in full_outs],
            scratch_shapes=scratch,
        ),
        compiler_params=pltpu.CompilerParams(
            dimension_semantics=("arbitrary",), vmem_limit_bytes=48 * 1024 * 1024
        ),
        cost_estimate=pl.CostEstimate(flops=flops, bytes_accessed=moved, transcendentals=0),
    )(*row_args, *full_args)


def flip_pairs(size, bit):
    return [(index, index ^ bit) for index in range(size)]


def flip(index, bit):
    return index + bit - 2 * bit * (lax.div(index, bit) % 2)


def send(src, dst, sems, slot, device):
    copy = pltpu.make_async_remote_copy(
        src_ref=src,
        dst_ref=dst,
        send_sem=sems.at[0, slot],
        recv_sem=sems.at[1, slot],
        device_id=device,
        device_id_type=pl.DeviceIdType.MESH,
    )
    copy.start()
    return copy


def exchange_kernel(chunks, orders, *refs):
    count = len(orders)
    term, blocks, refs = refs[0], refs[1 : 1 + count], refs[1 + count :]
    total, reduced, refs = refs[0], refs[1 : 1 + count], refs[1 + count :]
    core_got, y_sent, y_got, back_got, sems = refs[:5]
    scatter_refs = refs[5:]
    me = lax.axis_index("tensor")
    low = me % 2
    core_peer, y_peer = flip(me, 1), flip(me, 2)
    diagonal = flip(y_peer, 1)
    barrier = pltpu.get_barrier_semaphore()
    greeted = [{"tensor": core_peer}, {"tensor": y_peer}]
    if count:
        spot = lax.axis_index("dp")
        greeted.append({"tensor": diagonal})
        greeted += [{"dp": flip(spot, bit)} for bit in sorted(orders[0])]
    for device in greeted:
        pl.semaphore_signal(
            barrier, inc=1, device_id=device, device_id_type=pl.DeviceIdType.MESH
        )
    pl.semaphore_wait(barrier, len(greeted))

    half = term.shape[0] // 2
    size = half // chunks

    def rows(side, chunk):
        return pl.ds(pl.multiple_of(side * half + chunk * size, size), size)

    copies = []
    first = [
        send(term.at[rows(1 - low, c)], core_got.at[c], sems, c, {"tensor": core_peer})
        for c in range(chunks)
    ]
    copies += first

    state = []
    if count:
        scatter_sems = scatter_refs[-1]
        depth = len(orders[0])
        slot = 0
        for g, order in enumerate(orders):
            own = scatter_refs[g * 2 * depth : (g + 1) * 2 * depth]
            state.append({"order": order, "got": own[:depth], "kept": own[depth:], "src": blocks[g]})

        def start_stage(g, stage):
            entry = state[g]
            bit = entry["order"][stage]
            mine = lax.div(spot, bit) % 2
            width = entry["src"].shape[0] // 2
            entry["copy"] = send(
                entry["src"].at[pl.ds((1 - mine) * width, width)],
                entry["got"][stage],
                scatter_sems,
                g * depth + stage,
                {"dp": flip(spot, bit)},
            )
            copies.append(entry["copy"])

        def finish_stage(g, stage):
            entry = state[g]
            mine = lax.div(spot, entry["order"][stage]) % 2
            width = entry["src"].shape[0] // 2
            entry["copy"].wait_recv()
            for item in range(width):
                added = entry["src"][mine * width + item].astype(F32)
                added = added + entry["got"][stage][item].astype(F32)
                if stage == depth - 1:
                    reduced[g][...] = added
                entry["kept"][stage][item] = added.astype(BF16)
            entry["src"] = entry["kept"][stage]

        for g in range(count):
            start_stage(g, 0)

    second = []
    for c in range(chunks):
        first[c].wait_recv()
        y_sent[c] = (term[rows(low, c), :].astype(F32) + core_got[c].astype(F32)).astype(BF16)
        second.append(send(y_sent.at[c], y_got.at[c], sems, chunks + c, {"tensor": y_peer}))
    copies += second
    if count:
        for g in range(count):
            finish_stage(g, 0)
            if depth > 1:
                start_stage(g, 1)
    third = []
    for c in range(chunks):
        second[c].wait_recv()
        mine = rows(low, c)
        total[mine, :] = (y_sent[c].astype(F32) + y_got[c].astype(F32)).astype(BF16)
        third.append(send(total.at[mine], back_got.at[c], sems, 2 * chunks + c, {"tensor": core_peer}))
    copies += third
    for stage in range(1, depth if count else 1):
        for g in range(count):
            finish_stage(g, stage)
            if stage + 1 < depth:
                start_stage(g, stage + 1)
    if count:
        shared, shared_got = state[-1]["kept"][-1], scatter_refs[-2]
        final = [
            send(shared.at[0], shared_got.at[d], scatter_sems, count * depth + d, {"tensor": peer})
            for d, peer in enumerate((core_peer, y_peer, diagonal))
        ]
        copies += final
    for c in range(chunks):
        third[c].wait_recv()
        total[rows(1 - low, c), :] = back_got[c]
    if count:
        for copy in final:
            copy.wait_recv()
        pair = shared[0].astype(F32) + shared_got[0].astype(F32)
        reduced[-1][...] = pair + (shared_got[1].astype(F32) + shared_got[2].astype(F32))
    for copy in copies:
        copy.wait_send()


def sum_tensor(term, tensor_size, collective, blocks=(), orders=()):
    assert tensor_size == 4
    tok_count, model = term.shape
    chunks = 4
    size = tok_count // 2 // chunks
    buffers = [pltpu.VMEM((chunks, size, model), BF16)] * 4
    scratch = buffers + [pltpu.SemaphoreType.DMA((2, 3 * chunks))]
    outs = [jax.ShapeDtypeStruct(term.shape, BF16)]
    if blocks:
        depth = len(orders[0])
        for part in blocks:
            block = part.shape[1:]
            widths = [part.shape[0] >> (stage + 1) for stage in range(depth)]
            scratch += [pltpu.VMEM((width,) + block, BF16) for width in widths] * 2
            outs.append(jax.ShapeDtypeStruct(block, F32))
        scratch.append(pltpu.VMEM((3,) + blocks[-1].shape[1:], BF16))
        scratch.append(pltpu.SemaphoreType.DMA((2, len(blocks) * depth + 3)))
    result = pl.pallas_call(
        functools.partial(exchange_kernel, chunks, orders),
        name="exchange%d" % collective,
        out_shape=tuple(outs),
        in_specs=[pl.BlockSpec(memory_space=pltpu.VMEM)] * (1 + len(blocks)),
        out_specs=tuple(pl.BlockSpec(memory_space=pltpu.VMEM) for _ in outs),
        scratch_shapes=scratch,
        compiler_params=pltpu.CompilerParams(
            collective_id=collective, has_side_effects=True, vmem_limit_bytes=40 * 1024 * 1024
        ),
        cost_estimate=pl.CostEstimate(
            flops=16 * tok_count * model * 640, bytes_accessed=4 * term.size, transcendentals=0
        ),
    )(term, *blocks)
    return result if blocks else result[0]


def scatter_dp(blocks, size):
    index = lax.axis_index("dp")
    rows, cols = blocks.shape[1:]
    total = blocks
    bit = 1
    while bit < size:
        low = lax.rem(lax.div(index, bit), 2)
        parts = total.reshape(-1, 2, rows, cols)
        sent = lax.optimization_barrier(
            lax.dynamic_index_in_dim(parts, 1 - low, 1, keepdims=False).astype(jnp.bfloat16)
        )
        kept = lax.dynamic_index_in_dim(parts, low, 1, keepdims=False)
        got = lax.ppermute(sent, "dp", flip_pairs(size, bit))
        total = kept.astype(jnp.float32) + got.astype(jnp.float32)
        bit *= 2
    return total.reshape(rows, cols)


def on_device(
    tensor_size,
    dp_size,
    tokens,
    segment_ids,
    input_gain,
    q_weight,
    k_weight,
    v_weight,
    query_gain,
    key_gain,
    o_weight,
    post_attn_gain,
    pre_ffn_gain,
    gate_weight,
    up_weight,
    down_weight,
    post_ffn_gain,
    out_grad,
):
    tok_count, model = tokens.shape
    head_dim = k_weight.shape[1]
    units = gate_weight.shape[1]
    steps = tok_count // ROWS
    segments = segment_ids[0]
    row_index = jnp.arange(tok_count, dtype=jnp.int32)
    starts = jnp.sum((segments[None, :] < segments[:, None]).astype(jnp.int32), axis=1, keepdims=True)
    positions = row_index[:, None] - starts
    low = jnp.maximum(starts, row_index[:, None] - (WIN - 1))
    frequency = rope_base ** (-(jnp.arange(head_dim // 2, dtype=F32) * 2.0 / head_dim))
    angles = positions.astype(F32) * frequency[None, :]
    cosine, sine_tab = jnp.cos(angles), jnp.sin(angles)
    in_gain, pa_gain, pre_gain, pf_gain, q_gain, k_gain = (
        g[None, :]
        for g in (input_gain, post_attn_gain, pre_ffn_gain, post_ffn_gain, query_gain, key_gain)
    )
    square = tok_count * model * head_dim
    attend_full = (in_gain, q_weight, k_weight, v_weight, q_gain, k_gain, o_weight)
    wide = (tok_count, model)
    heads = (tok_count, head_dim)
    padded = (tok_count + WIN, head_dim)

    def attend(tok, cos_b, sin_b, low_b, gain, q_w, k_w, v_w, qg, kg, o_w,
               term, attn, q_rot, stats, q_unit, k_unit, k_pad, v_pad):
        attend_kernel(tok, gain, q_w, k_w, v_w, qg, kg, o_w, cos_b, sin_b, low_b,
                      term, attn, q_rot, k_pad, v_pad, stats, q_unit, k_unit)

    term, attn, q_rot, stats, q_unit, k_unit, k_pad, v_pad = row_call(
        attend, "attend", steps, (tokens, cosine, sine_tab, low), attend_full,
        ((wide, BF16), (heads, BF16), (heads, BF16), ((tok_count, 128), F32), (heads, F32), (heads, F32)),
        ((padded, BF16), (padded, BF16)), (), 14 * square, False,
    )
    attn_sum = sum_tensor(term, tensor_size, 0)
    hidden_shape = (tok_count, units)
    term, gate, up = row_call(
        ffn_kernel, "ffn", steps, (tokens, attn_sum),
        (pa_gain, pre_gain, gate_weight, up_weight, down_weight),
        ((wide, BF16), (hidden_shape, F32), (hidden_shape, F32)), (), (), 12 * square, False,
    )
    ffn_sum = sum_tensor(term, tensor_size, 1)
    output, term, early, ffn_gains = row_call(
        ffn_back_kernel, "ffn_back", steps, (tokens, attn_sum, ffn_sum, out_grad, gate, up),
        (pa_gain, pre_gain, pf_gain, gate_weight, up_weight, down_weight),
        ((wide, BF16), (wide, BF16)), (((model, 3 * units), BF16), ((8, model), F32)),
        (pltpu.VMEM((model, 3 * units), F32),), 24 * square, False,
    )
    part_rows = model // dp_size
    early = scatter_dp(early.reshape(dp_size, part_rows, 3 * units), dp_size)
    ffn_back = sum_tensor(term, tensor_size, 2)
    term, late, attn_gains, head_gains = row_call(
        attend_back_kernel, "attend_back", steps,
        (tokens, out_grad, ffn_back, attn_sum, attn, q_rot, stats, q_unit, k_unit, cosine, sine_tab, low),
        (k_pad, v_pad, pa_gain, in_gain, q_gain, k_gain, q_weight, k_weight, v_weight, o_weight),
        ((wide, BF16),), (((model, 4 * head_dim), BF16), ((8, model), F32), ((8, head_dim), F32)),
        (pltpu.VMEM((model, 4 * head_dim), F32), pltpu.VMEM(padded, F32), pltpu.VMEM(padded, F32)),
        30 * square, True,
    )
    gains = jnp.concatenate(
        [
            attn_gains[0] / tensor_size,
            ffn_gains[0] / tensor_size,
            attn_gains[1],
            ffn_gains[1],
            head_gains[0],
            head_gains[1],
        ]
    )
    gain_count = gains.shape[0]
    cols = 2 * head_dim
    gain_rows = -(-gain_count // (16 * cols)) * 16
    gains = jnp.pad(gains, (0, gain_rows * cols - gain_count)).reshape(1, gain_rows, cols)
    gains = jnp.broadcast_to(gains.astype(BF16), (dp_size, gain_rows, cols))
    late = late.reshape(dp_size, part_rows, 2 * cols)
    bits = dp_size.bit_length() - 1
    plain = tuple(1 << k for k in range(bits))
    orders = (plain, plain[1::-1] + plain[2:])

    def ordered(part, order):
        shape = (2,) * bits + part.shape[1:]
        axes = tuple(bits - bit.bit_length() for bit in order) + (bits, bits + 1)
        return part.reshape(shape).transpose(axes).reshape(part.shape)

    blocks = (
        ordered(late[:, :, :cols], orders[0]),
        ordered(jnp.concatenate([late[:, :, cols:], gains], axis=1), orders[1]),
    )
    attn_back, first_part, shared = sum_tensor(term, tensor_size, 3, blocks, orders)
    grad_tokens = out_grad.astype(F32) + ffn_back.astype(F32) + attn_back.astype(F32)
    grad_o_w = first_part[:, :head_dim]
    grad_q_w = first_part[:, head_dim:]
    grad_k_w = shared[:part_rows, :head_dim]
    grad_v_w = shared[:part_rows, head_dim:]
    gain_sum = shared[part_rows:].reshape(-1)
    grad_post_attn = gain_sum[:model]
    grad_post_ffn = gain_sum[model : 2 * model]
    grad_input_gain = gain_sum[2 * model : 3 * model]
    grad_pre_ffn = gain_sum[3 * model : 4 * model]
    grad_query_gain = gain_sum[4 * model : 4 * model + head_dim]
    grad_key_gain = gain_sum[4 * model + head_dim : gain_count]
    grad_gate_w = early[:, :units]
    grad_up_w = early[:, units : 2 * units]
    grad_down_w = early[:, 2 * units :]
    return (
        output, grad_tokens, grad_input_gain, grad_q_w, grad_k_w, grad_v_w, grad_query_gain,
        grad_key_gain, grad_o_w, grad_post_attn, grad_pre_ffn, grad_gate_w, grad_up_w, grad_down_w,
        grad_post_ffn,
    )


def solution(mesh):
    in_specs = (
        P("dp", None),
        P("dp", None),
        P(),
        P(None, "tensor"),
        P(),
        P(),
        P(),
        P(),
        P(None, "tensor"),
        P(),
        P(),
        P(None, "tensor"),
        P(None, "tensor"),
        P(None, "tensor"),
        P(),
        P("dp", None),
    )
    out_specs = (
        P("dp", None),
        P("dp", None),
        P(),
        P("dp", "tensor"),
        P("dp", None),
        P("dp", None),
        P(),
        P(),
        P("dp", "tensor"),
        P(),
        P(),
        P("dp", "tensor"),
        P("dp", "tensor"),
        P("dp", "tensor"),
        P(),
    )
    body = functools.partial(on_device, mesh.shape["tensor"], mesh.shape["dp"])
    return jax.shard_map(
        body, mesh=mesh, in_specs=in_specs, out_specs=out_specs, check_vma=False
    )
```

```python
import functools

import jax
import jax.numpy as jnp
from jax import lax
from jax.experimental import pallas as pl
from jax.experimental.pallas import tpu as pltpu
from jax.sharding import PartitionSpec as P

WIN = 512
ROWS = 256


norm_eps = 1e-06
rope_base = 10000.0
gelu_coef = 0.7978845608028654
cube_coef = 0.044715
masked_value = -1e30
contract_rows = (((0,), (0,)), ((), ()))
contract_cols = (((1,), (1,)), ((), ()))
F32 = jnp.float32
BF16 = jnp.bfloat16


def mat(left, right):
    return jnp.dot(left, right, preferred_element_type=F32)


def mat_rows(left, right):
    return lax.dot_general(left, right, contract_rows, preferred_element_type=F32)


def mat_cols(left, right):
    return lax.dot_general(left, right, contract_cols, preferred_element_type=F32)


def rms_unit(values):
    inverse = lax.rsqrt(jnp.mean(values * values, axis=-1, keepdims=True) + norm_eps)
    return (values * inverse, inverse)


def rms_backward(grad_vals, unit_vals, inverse, gain_vec):
    scaled = grad_vals * (1.0 + gain_vec)
    return inverse * (scaled - unit_vals * jnp.mean(scaled * unit_vals, axis=-1, keepdims=True))


def rotate(values, cosine, sine_tab, sign):
    half_dim = values.shape[-1] // 2
    first = values[:, :half_dim]
    second = values[:, half_dim:]
    return jnp.concatenate(
        [first * cosine - sign * second * sine_tab, second * cosine + sign * first * sine_tab],
        axis=-1,
    )


def column_sum(values):
    return jnp.sum(values, axis=0, keepdims=True)


def allowed_keys(low_col, block):
    rows = low_col.shape[0]
    col_ids = lax.broadcasted_iota(jnp.int32, (rows, rows + WIN), 1) - WIN
    row_ids = lax.broadcasted_iota(jnp.int32, (rows, rows + WIN), 0)
    return (col_ids >= low_col - block * rows) & (col_ids <= row_ids)


def attend_kernel(
    tok, gain, q_w, k_w, v_w, q_gain, k_gain, o_w, cosine, sine_tab, low,
    term, attn, q_rot, k_pad, v_pad, stats, q_unit, k_unit,
):
    block = pl.program_id(0)
    rows, head_dim = attn.shape

    @pl.when(block == 0)
    def _():
        k_pad[:WIN, :] = jnp.zeros((WIN, head_dim), BF16)
        v_pad[:WIN, :] = jnp.zeros((WIN, head_dim), BF16)

    unit_in, _ = rms_unit(tok[...].astype(F32))
    normed = (unit_in * (1.0 + gain[...])).astype(BF16)
    cos_b, sin_b = cosine[...], sine_tab[...]
    q_u, q_inv = rms_unit(mat(normed, q_w[...]))
    k_u, k_inv = rms_unit(mat(normed, k_w[...]))
    q_unit[...] = q_u
    k_unit[...] = k_u
    q_r = rotate(q_u * (1.0 + q_gain[...]), cos_b, sin_b, 1.0).astype(BF16)
    q_rot[...] = q_r
    here = pl.ds(pl.multiple_of(block * rows + WIN, rows), rows)
    span = pl.ds(pl.multiple_of(block * rows, rows), rows + WIN)
    k_pad[here, :] = rotate(k_u * (1.0 + k_gain[...]), cos_b, sin_b, 1.0).astype(BF16)
    v_pad[here, :] = mat(normed, v_w[...]).astype(BF16)
    scores = mat_cols(q_r, k_pad[span, :]) * (head_dim ** (-0.5))
    scores = jnp.where(allowed_keys(low[...], block), scores, masked_value)
    row_max = jnp.max(scores, axis=-1, keepdims=True)
    exp_vals = jnp.exp(scores - row_max)
    row_total = jnp.sum(exp_vals, axis=-1, keepdims=True)
    probs = (exp_vals * (1.0 / row_total)).astype(BF16)
    result = mat(probs, v_pad[span, :]).astype(BF16)
    attn[...] = result
    term[...] = mat_cols(result, o_w[...]).astype(BF16)
    lane = lax.broadcasted_iota(jnp.int32, stats.shape, 1)
    lse = row_max + jnp.log(row_total)
    stats[...] = jnp.where(lane == 0, lse, jnp.where(lane == 1, q_inv, k_inv))


def middle(tok, attn_sum, post_attn_gain):
    attn_unit, attn_inv = rms_unit(attn_sum[...].astype(F32))
    hidden = tok[...].astype(F32) + attn_unit * (1.0 + post_attn_gain[...])
    mid_unit, mid_inv = rms_unit(hidden)
    return (attn_unit, attn_inv, hidden, mid_unit, mid_inv)


def ffn_kernel(tok, attn_sum, pa_gain, pre_gain, gate_w, up_w, down_w, term, gate, up):
    _, _, _, mid_unit, _ = middle(tok, attn_sum, pa_gain)
    normed = (mid_unit * (1.0 + pre_gain[...])).astype(BF16)
    gate_pre = mat(normed, gate_w[...])
    up_pre = mat(normed, up_w[...])
    gate[...] = gate_pre
    up[...] = up_pre
    tanh_val = jnp.tanh(gelu_coef * (gate_pre + cube_coef * gate_pre * gate_pre * gate_pre))
    act = (0.5 * gate_pre * (1.0 + tanh_val) * up_pre).astype(BF16)
    term[...] = mat_cols(act, down_w[...]).astype(BF16)


def ffn_back_kernel(
    tok, attn_sum, ffn_sum, out_grad, gate, up, pa_gain, pre_gain, pf_gain, gate_w, up_w, down_w,
    output, term, weight_grads, gains, total,
):
    block = pl.program_id(0)

    @pl.when(block == 0)
    def _():
        total[...] = jnp.zeros_like(total)
        gains[...] = jnp.zeros_like(gains)

    _, _, hidden, mid_unit, mid_inv = middle(tok, attn_sum, pa_gain)
    normed = (mid_unit * (1.0 + pre_gain[...])).astype(BF16)
    ffn_unit, ffn_inv = rms_unit(ffn_sum[...].astype(F32))
    output[...] = (hidden + ffn_unit * (1.0 + pf_gain[...])).astype(BF16)
    grad_out = out_grad[...].astype(F32)
    gains[0:1, :] += column_sum(grad_out * ffn_unit)
    grad_sum = rms_backward(grad_out, ffn_unit, ffn_inv, pf_gain[...]).astype(BF16)
    grad_act = mat(grad_sum, down_w[...])
    gate_pre, up_pre = gate[...], up[...]
    squared = gate_pre * gate_pre
    tanh_val = jnp.tanh(gelu_coef * (gate_pre + cube_coef * squared * gate_pre))
    gelu_value = 0.5 * gate_pre * (1.0 + tanh_val)
    slope = 0.5 * (1.0 + tanh_val) + 0.5 * gate_pre * (1.0 - tanh_val * tanh_val) * gelu_coef * (
        1.0 + 3.0 * cube_coef * squared
    )
    act = (gelu_value * up_pre).astype(BF16)
    grad_gate = (grad_act * up_pre * slope).astype(BF16)
    grad_up = (grad_act * gelu_value).astype(BF16)
    units = gate_pre.shape[1]
    total[:, :units] += mat_rows(normed, grad_gate)
    total[:, units : 2 * units] += mat_rows(normed, grad_up)
    total[:, 2 * units :] += mat_rows(grad_sum, act)
    grad_mid = mat_cols(grad_gate, gate_w[...]) + mat_cols(grad_up, up_w[...])
    gains[1:2, :] += column_sum(grad_mid * mid_unit)
    term[...] = rms_backward(grad_mid, mid_unit, mid_inv, pre_gain[...]).astype(BF16)

    @pl.when(block == pl.num_programs(0) - 1)
    def _():
        weight_grads[...] = total[...].astype(BF16)


def attend_back_kernel(
    tok, out_grad, ffn_back, attn_sum, attn, q_rot, stats, q_unit, k_unit, cosine, sine_tab, low,
    k_pad, v_pad, pa_gain, in_gain, q_gain, k_gain, q_w, k_w, v_w, o_w,
    term, weight_grads, gains, head_gains, total, grad_k, grad_v,
):
    step = pl.program_id(0)
    block = pl.num_programs(0) - 1 - step
    rows, head_dim = attn.shape
    scale = head_dim ** (-0.5)

    @pl.when(step == 0)
    def _():
        for ref in (total, gains, head_gains, grad_k, grad_v):
            ref[...] = jnp.zeros_like(ref)

    attn_unit, attn_inv = rms_unit(attn_sum[...].astype(F32))
    grad_hidden = out_grad[...].astype(F32) + ffn_back[...].astype(F32)
    gains[0:1, :] += column_sum(grad_hidden * attn_unit)
    grad_sum = rms_backward(grad_hidden, attn_unit, attn_inv, pa_gain[...]).astype(BF16)
    grad_attn = mat(grad_sum, o_w[...]).astype(BF16)
    attn_vals = attn[...]
    total[:, :head_dim] += mat_rows(grad_sum, attn_vals)
    delta = jnp.sum(grad_attn.astype(F32) * attn_vals.astype(F32), axis=-1, keepdims=True)
    span = pl.ds(pl.multiple_of(block * rows, rows), rows + WIN)
    here = pl.ds(pl.multiple_of(block * rows + WIN, rows), rows)
    q_r = q_rot[...]
    k_span, v_span = k_pad[span, :], v_pad[span, :]
    scores = mat_cols(q_r, k_span) * scale
    allowed = allowed_keys(low[...], block)
    probs = jnp.exp(jnp.where(allowed, scores - stats[:, 0:1], masked_value))
    grad_probs = mat_cols(grad_attn, v_span)
    grad_scores = (probs * (grad_probs - delta) * scale).astype(BF16)
    grad_query = mat(grad_scores, k_span)
    grad_k[span, :] += mat_rows(grad_scores, q_r)
    grad_v[span, :] += mat_rows(probs.astype(BF16), grad_attn)
    cos_b, sin_b = cosine[...], sine_tab[...]
    grad_q_unit = rotate(grad_query, cos_b, sin_b, -1.0)
    grad_k_unit = rotate(grad_k[here, :], cos_b, sin_b, -1.0)
    q_u, k_u = q_unit[...], k_unit[...]
    head_gains[0:1, :] += column_sum(grad_q_unit * q_u)
    head_gains[1:2, :] += column_sum(grad_k_unit * k_u)
    grad_q_bf = rms_backward(grad_q_unit, q_u, stats[:, 1:2], q_gain[...]).astype(BF16)
    grad_k_bf = rms_backward(grad_k_unit, k_u, stats[:, 2:3], k_gain[...]).astype(BF16)
    grad_v_bf = grad_v[here, :].astype(BF16)
    unit_in, inv_in = rms_unit(tok[...].astype(F32))
    normed = (unit_in * (1.0 + in_gain[...])).astype(BF16)
    total[:, head_dim : 2 * head_dim] += mat_rows(normed, grad_q_bf)
    total[:, 2 * head_dim : 3 * head_dim] += mat_rows(normed, grad_k_bf)
    total[:, 3 * head_dim :] += mat_rows(normed, grad_v_bf)
    grad_in = mat_cols(grad_q_bf, q_w[...]) + mat_cols(grad_k_bf, k_w[...])
    grad_in = grad_in + mat_cols(grad_v_bf, v_w[...])
    gains[1:2, :] += column_sum(grad_in * unit_in)
    term[...] = rms_backward(grad_in, unit_in, inv_in, in_gain[...]).astype(BF16)

    @pl.when(block == 0)
    def _():
        weight_grads[...] = total[...].astype(BF16)


def row_call(kernel, name, steps, row_args, full_args, row_outs, full_outs, scratch, flops, reverse):
    def row_map(i):
        return (steps - 1 - i if reverse else i, 0)

    def full_map(i):
        return (0, 0)

    def row_spec(shape):
        return pl.BlockSpec((shape[0] // steps, shape[1]), row_map)

    def full_spec(shape):
        return pl.BlockSpec(shape, full_map)

    moved = sum(x.size * x.dtype.itemsize for x in tuple(row_args) + tuple(full_args))
    return pl.pallas_call(
        kernel,
        name=name,
        out_shape=tuple(jax.ShapeDtypeStruct(s, d) for s, d in tuple(row_outs) + tuple(full_outs)),
        grid_spec=pltpu.PrefetchScalarGridSpec(
            num_scalar_prefetch=0,
            grid=(steps,),
            in_specs=[row_spec(x.shape) for x in row_args] + [full_spec(x.shape) for x in full_args],
            out_specs=[row_spec(s) for s, _ in row_outs] + [full_spec(s) for s, _ in full_outs],
            scratch_shapes=scratch,
        ),
        compiler_params=pltpu.CompilerParams(
            dimension_semantics=("arbitrary",), vmem_limit_bytes=32 * 1024 * 1024
        ),
        cost_estimate=pl.CostEstimate(flops=flops, bytes_accessed=moved, transcendentals=0),
    )(*row_args, *full_args)


def flip(index, bit):
    return index + bit - 2 * bit * (lax.div(index, bit) % 2)


def send(src, dst, sems, slot, device):
    copy = pltpu.make_async_remote_copy(
        src_ref=src,
        dst_ref=dst,
        send_sem=sems.at[0, slot],
        recv_sem=sems.at[1, slot],
        device_id=device,
        device_id_type=pl.DeviceIdType.MESH,
    )
    copy.start()
    return copy


def exchange_kernel(chunks, orders, closing, *refs):
    count = len(orders)
    term, blocks, refs = refs[0], refs[1 : 1 + count], refs[1 + count :]
    total, reduced, refs = refs[0], refs[1 : 1 + count], refs[1 + count :]
    core_got, y_sent, y_got, back_got, sems = refs[:5]
    scatter_refs = refs[5:]
    me = lax.axis_index("tensor")
    low = me % 2
    core_peer, y_peer = flip(me, 1), flip(me, 2)
    diagonal = flip(y_peer, 1)
    barrier = pltpu.get_barrier_semaphore()
    greeted = [{"tensor": core_peer}, {"tensor": y_peer}]
    if closing:
        greeted.append({"tensor": diagonal})
    if count:
        spot = lax.axis_index("dp")
        greeted += [{"dp": flip(spot, bit)} for bit in sorted(set(sum(orders, ())))]
    for device in greeted:
        pl.semaphore_signal(
            barrier, inc=1, device_id=device, device_id_type=pl.DeviceIdType.MESH
        )
    pl.semaphore_wait(barrier, len(greeted))

    half = term.shape[0] // 2
    size = half // chunks

    def rows(side, chunk):
        return pl.ds(pl.multiple_of(side * half + chunk * size, size), size)

    copies = []
    first = [
        send(term.at[rows(1 - low, c)], core_got.at[c], sems, c, {"tensor": core_peer})
        for c in range(chunks)
    ]
    copies += first

    state = []
    if count:
        scatter_sems = scatter_refs[-1]
        slots = 0
        used = 0
        for g, order in enumerate(orders):
            depth = len(order)
            got = scatter_refs[used : used + depth]
            kept = scatter_refs[used + depth : used + 2 * depth]
            used += 2 * depth
            state.append(
                {"depth": depth, "order": order, "got": got, "kept": kept, "src": blocks[g], "slot": slots}
            )
            slots += depth
        deepest = max(len(order) for order in orders)

        def start_stage(g, stage):
            entry = state[g]
            bit = entry["order"][stage]
            mine = lax.div(spot, bit) % 2
            width = entry["src"].shape[0] // 2
            entry["copy"] = send(
                entry["src"].at[pl.ds((1 - mine) * width, width)],
                entry["got"][stage],
                scatter_sems,
                entry["slot"] + stage,
                {"dp": flip(spot, bit)},
            )
            copies.append(entry["copy"])

        def finish_stage(g, stage):
            entry = state[g]
            mine = lax.div(spot, entry["order"][stage]) % 2
            width = entry["src"].shape[0] // 2
            entry["copy"].wait_recv()
            for item in range(width):
                added = entry["src"][mine * width + item].astype(F32)
                added = added + entry["got"][stage][item].astype(F32)
                if stage < entry["depth"] - 1:
                    entry["kept"][stage][item] = added.astype(BF16)
                elif not closing:
                    reduced[g][item] = added.astype(BF16)
                elif g < count - 1:
                    reduced[g][...] = added
                else:
                    entry["kept"][stage][item] = added.astype(BF16)
            entry["src"] = entry["kept"][stage]

        for g in range(count):
            start_stage(g, 0)

    second = []
    for c in range(chunks):
        first[c].wait_recv()
        y_sent[c] = (term[rows(low, c), :].astype(F32) + core_got[c].astype(F32)).astype(BF16)
        second.append(send(y_sent.at[c], y_got.at[c], sems, chunks + c, {"tensor": y_peer}))
    copies += second
    if count:
        for g in range(count):
            finish_stage(g, 0)
            if state[g]["depth"] > 1:
                start_stage(g, 1)
    third = []
    for c in range(chunks):
        second[c].wait_recv()
        mine = rows(low, c)
        total[mine, :] = (y_sent[c].astype(F32) + y_got[c].astype(F32)).astype(BF16)
        third.append(send(total.at[mine], back_got.at[c], sems, 2 * chunks + c, {"tensor": core_peer}))
    copies += third
    for stage in range(1, deepest if count else 1):
        for g in range(count):
            if stage < state[g]["depth"]:
                finish_stage(g, stage)
            if stage + 1 < state[g]["depth"]:
                start_stage(g, stage + 1)
    if closing:
        shared, shared_got = state[-1]["kept"][-1], scatter_refs[-2]
        final = [
            send(shared.at[0], shared_got.at[d], scatter_sems, slots + d, {"tensor": peer})
            for d, peer in enumerate((core_peer, y_peer, diagonal))
        ]
        copies += final
    for c in range(chunks):
        third[c].wait_recv()
        total[rows(1 - low, c), :] = back_got[c]
    if closing:
        for copy in final:
            copy.wait_recv()
        pair = shared[0].astype(F32) + shared_got[0].astype(F32)
        reduced[-1][...] = pair + (shared_got[1].astype(F32) + shared_got[2].astype(F32))
    for copy in copies:
        copy.wait_send()


def sum_tensor(term, tensor_size, collective, blocks=(), orders=(), closing=False):
    assert tensor_size == 4
    tok_count, model = term.shape
    chunks = 4
    size = tok_count // 2 // chunks
    buffers = [pltpu.VMEM((chunks, size, model), BF16)] * 4
    scratch = buffers + [pltpu.SemaphoreType.DMA((2, 3 * chunks))]
    outs = [jax.ShapeDtypeStruct(term.shape, BF16)]
    if blocks:
        for part, order in zip(blocks, orders):
            block = part.shape[1:]
            widths = [part.shape[0] >> (stage + 1) for stage in range(len(order))]
            scratch += [pltpu.VMEM((width,) + block, BF16) for width in widths] * 2
            shape = block if closing else (widths[-1],) + block
            outs.append(jax.ShapeDtypeStruct(shape, F32 if closing else BF16))
        if closing:
            scratch.append(pltpu.VMEM((3,) + blocks[-1].shape[1:], BF16))
        slots = sum(len(order) for order in orders) + (3 if closing else 0)
        scratch.append(pltpu.SemaphoreType.DMA((2, slots)))
    result = pl.pallas_call(
        functools.partial(exchange_kernel, chunks, orders, closing),
        name="exchange%d" % collective,
        out_shape=tuple(outs),
        in_specs=[pl.BlockSpec(memory_space=pltpu.VMEM)] * (1 + len(blocks)),
        out_specs=tuple(pl.BlockSpec(memory_space=pltpu.VMEM) for _ in outs),
        scratch_shapes=scratch,
        compiler_params=pltpu.CompilerParams(
            collective_id=collective, has_side_effects=True,
            vmem_limit_bytes=(24 if blocks else 10) * 1024 * 1024
        ),
        cost_estimate=pl.CostEstimate(
            flops=16 * tok_count * model * 640, bytes_accessed=4 * term.size, transcendentals=0
        ),
    )(term, *blocks)
    return result if blocks else result[0]


def on_device(
    tensor_size,
    dp_size,
    tokens,
    segment_ids,
    input_gain,
    q_weight,
    k_weight,
    v_weight,
    query_gain,
    key_gain,
    o_weight,
    post_attn_gain,
    pre_ffn_gain,
    gate_weight,
    up_weight,
    down_weight,
    post_ffn_gain,
    out_grad,
):
    tok_count, model = tokens.shape
    head_dim = k_weight.shape[1]
    units = gate_weight.shape[1]
    steps = tok_count // ROWS
    segments = segment_ids[0]
    row_index = jnp.arange(tok_count, dtype=jnp.int32)
    starts = jnp.sum((segments[None, :] < segments[:, None]).astype(jnp.int32), axis=1, keepdims=True)
    positions = row_index[:, None] - starts
    low = jnp.maximum(starts, row_index[:, None] - (WIN - 1))
    frequency = rope_base ** (-(jnp.arange(head_dim // 2, dtype=F32) * 2.0 / head_dim))
    angles = positions.astype(F32) * frequency[None, :]
    cosine, sine_tab = jnp.cos(angles), jnp.sin(angles)
    in_gain, pa_gain, pre_gain, pf_gain, q_gain, k_gain = (
        g[None, :]
        for g in (input_gain, post_attn_gain, pre_ffn_gain, post_ffn_gain, query_gain, key_gain)
    )
    square = tok_count * model * head_dim
    attend_full = (in_gain, q_weight, k_weight, v_weight, q_gain, k_gain, o_weight)
    wide = (tok_count, model)
    heads = (tok_count, head_dim)
    padded = (tok_count + WIN, head_dim)

    def attend(tok, cos_b, sin_b, low_b, gain, q_w, k_w, v_w, qg, kg, o_w,
               term, attn, q_rot, stats, q_unit, k_unit, k_pad, v_pad):
        attend_kernel(tok, gain, q_w, k_w, v_w, qg, kg, o_w, cos_b, sin_b, low_b,
                      term, attn, q_rot, k_pad, v_pad, stats, q_unit, k_unit)

    term, attn, q_rot, stats, q_unit, k_unit, k_pad, v_pad = row_call(
        attend, "attend", steps, (tokens, cosine, sine_tab, low), attend_full,
        ((wide, BF16), (heads, BF16), (heads, BF16), ((tok_count, 128), F32), (heads, F32), (heads, F32)),
        ((padded, BF16), (padded, BF16)), (), 14 * square, False,
    )
    attn_sum = sum_tensor(term, tensor_size, 0)
    hidden_shape = (tok_count, units)
    term, gate, up = row_call(
        ffn_kernel, "ffn", steps, (tokens, attn_sum),
        (pa_gain, pre_gain, gate_weight, up_weight, down_weight),
        ((wide, BF16), (hidden_shape, F32), (hidden_shape, F32)), (), (), 12 * square, False,
    )
    ffn_sum = sum_tensor(term, tensor_size, 1)
    output, term, early, ffn_gains = row_call(
        ffn_back_kernel, "ffn_back", steps, (tokens, attn_sum, ffn_sum, out_grad, gate, up),
        (pa_gain, pre_gain, pf_gain, gate_weight, up_weight, down_weight),
        ((wide, BF16), (wide, BF16)), (((model, 3 * units), BF16), ((8, model), F32)),
        (pltpu.VMEM((model, 3 * units), F32),), 24 * square, False,
    )
    part_rows = model // dp_size
    bits = dp_size.bit_length() - 1
    plain = tuple(1 << k for k in range(bits))
    orders = (plain, plain[1::-1] + plain[2:])

    def ordered(part, order):
        shape = (2,) * bits + part.shape[1:]
        axes = tuple(bits - bit.bit_length() for bit in order) + (bits, bits + 1)
        return part.reshape(shape).transpose(axes).reshape(part.shape)

    early = early.reshape(dp_size, part_rows, 3 * units)
    side = 3 * units // 2
    ffn_back, early_a, early_b = sum_tensor(
        term, tensor_size, 2,
        (ordered(early[:, :, :side], orders[0]), ordered(early[:, :, side:], orders[1])),
        (orders[0][:2], orders[1][:2]),
    )
    term, late, attn_gains, head_gains = row_call(
        attend_back_kernel, "attend_back", steps,
        (tokens, out_grad, ffn_back, attn_sum, attn, q_rot, stats, q_unit, k_unit, cosine, sine_tab, low),
        (k_pad, v_pad, pa_gain, in_gain, q_gain, k_gain, q_weight, k_weight, v_weight, o_weight),
        ((wide, BF16),), (((model, 4 * head_dim), BF16), ((8, model), F32), ((8, head_dim), F32)),
        (pltpu.VMEM((model, 4 * head_dim), F32), pltpu.VMEM(padded, F32), pltpu.VMEM(padded, F32)),
        30 * square, True,
    )
    gains = jnp.concatenate(
        [
            attn_gains[0] / tensor_size,
            ffn_gains[0] / tensor_size,
            attn_gains[1],
            ffn_gains[1],
            head_gains[0],
            head_gains[1],
        ]
    )
    gain_count = gains.shape[0]
    cols = 2 * head_dim
    gain_rows = -(-gain_count // (16 * cols)) * 16
    gains = jnp.pad(gains, (0, gain_rows * cols - gain_count)).reshape(1, gain_rows, cols)
    gains = jnp.broadcast_to(gains.astype(BF16), (dp_size, gain_rows, cols))
    late = late.reshape(dp_size, part_rows, 2 * cols)
    blocks = (
        early_a,
        early_b,
        ordered(late[:, :, :cols], orders[0]),
        ordered(jnp.concatenate([late[:, :, cols:], gains], axis=1), orders[1]),
    )
    tails = (plain[2:], plain[2:]) + orders
    attn_back, early_a, early_b, first_part, shared = sum_tensor(
        term, tensor_size, 3, blocks, tails, True
    )
    early = jnp.concatenate([early_a, early_b], axis=1)
    grad_tokens = out_grad.astype(F32) + ffn_back.astype(F32) + attn_back.astype(F32)
    grad_o_w = first_part[:, :head_dim]
    grad_q_w = first_part[:, head_dim:]
    grad_k_w = shared[:part_rows, :head_dim]
    grad_v_w = shared[:part_rows, head_dim:]
    gain_sum = shared[part_rows:].reshape(-1)
    grad_post_attn = gain_sum[:model]
    grad_post_ffn = gain_sum[model : 2 * model]
    grad_input_gain = gain_sum[2 * model : 3 * model]
    grad_pre_ffn = gain_sum[3 * model : 4 * model]
    grad_query_gain = gain_sum[4 * model : 4 * model + head_dim]
    grad_key_gain = gain_sum[4 * model + head_dim : gain_count]
    grad_gate_w = early[:, :units]
    grad_up_w = early[:, units : 2 * units]
    grad_down_w = early[:, 2 * units :]
    return (
        output, grad_tokens, grad_input_gain, grad_q_w, grad_k_w, grad_v_w, grad_query_gain,
        grad_key_gain, grad_o_w, grad_post_attn, grad_pre_ffn, grad_gate_w, grad_up_w, grad_down_w,
        grad_post_ffn,
    )


def solution(mesh):
    in_specs = (
        P("dp", None),
        P("dp", None),
        P(),
        P(None, "tensor"),
        P(),
        P(),
        P(),
        P(),
        P(None, "tensor"),
        P(),
        P(),
        P(None, "tensor"),
        P(None, "tensor"),
        P(None, "tensor"),
        P(),
        P("dp", None),
    )
    out_specs = (
        P("dp", None),
        P("dp", None),
        P(),
        P("dp", "tensor"),
        P("dp", None),
        P("dp", None),
        P(),
        P(),
        P("dp", "tensor"),
        P(),
        P(),
        P("dp", "tensor"),
        P("dp", "tensor"),
        P("dp", "tensor"),
        P(),
    )
    body = functools.partial(on_device, mesh.shape["tensor"], mesh.shape["dp"])
    return jax.shard_map(
        body, mesh=mesh, in_specs=in_specs, out_specs=out_specs, check_vma=False
    )
```
